32 devices in a mesh: stream: 16 (over z, y, x), span: 2 (over core).
Axes of the slice: x: 2, y: 2, z: 4, core: 2. Of those that a mesh axis runs over, the one named last changes fastest.
Arguments:
- adjoint_start: float32 [5, 128, 32, 512], P(None, 'stream', 'span'), may hold values from -4 to 4
- source: float32 [5, 128, 32, 512], P(None, 'stream', 'span'), may hold values from -40 to 40
- flow_state: float32 [5, 128, 32, 512], P(None, 'stream', 'span'), may hold values from -4 to 4, as said below
- precond: float32 [5, 5, 128, 32, 512], P(None, None, 'stream', 'span'), may hold values from -0.12 to 0.2
- flux_jac: float32 [3, 5, 5], replicated, may hold values from -4 to 4
- bc_codes: int32 [128, 32], P('stream', 'span'), may hold values from 0 to 2
Outputs:
- adjoint: float32 [5, 128, 32, 512], P(None, 'stream', 'span')
- residual_rms: float32 [2], replicated
The draws below stay inside these ranges and needn't reach their ends.
Inputs may be any that keep to these rules, and one draw needn't show every extreme that they name: `bc_codes`: 0 is a wall, 1 a far field, 2 an extrapolation face. `flow_state`: density and pressure lie in 0.5 to 2.
All inputs are finite; a program needn't handle non-finite values.
Results may differ from the reference program's by a relative error of at most 0.0003.
Values sent between devices are 32-bit elements; how exact they have to be, the bound alone decides.
No kernel may reach another device: no remote copies, remote signals or barrier semaphores. Data moves between devices by JAX's collectives and lax.ppermute only.
A program may use at most 128 MiB of HBM per device.

```python
import jax
import jax.numpy as jnp
from jax import lax

NV = 5
SWEEPS = 2
NI = 128
NJ = 32
NK = 512


def draw_flow_state(key, part):
    keys = jax.random.split(key, 3)
    density = jax.random.uniform(keys[0], (1, NI, NJ, NK), jnp.float32, 0.5, 2.0)
    momentum = jax.random.truncated_normal(keys[1], -4.0, 4.0, (3, NI, NJ, NK), jnp.float32)
    pressure = jax.random.uniform(keys[2], (1, NI, NJ, NK), jnp.float32, 0.5, 2.0)
    return jnp.concatenate([density, momentum, pressure], axis=0)


def draw_source(key, part):
    keys = jax.random.split(key, 2)
    ramp = 10.0 ** (jnp.arange(NI, dtype=jnp.float32) / (NI - 1))
    column = 10.0 ** jax.random.uniform(keys[1], (NJ,), jnp.float32, 0.0, 1.0)
    base = jax.random.truncated_normal(keys[0], -4.0, 4.0, (NV, NI, NJ, NK), jnp.float32)
    return 0.1 * base * ramp[None, :, None, None] * column[None, None, :, None]


def draw_precond(key, part):
    keys = jax.random.split(key, 2)
    diagonal = jax.random.uniform(keys[0], (NV, NI, NJ, NK), jnp.float32, 0.08, 0.2)
    offdiag = 0.03 * jax.random.truncated_normal(keys[1], -4.0, 4.0, (NV, NV, NI, NJ, NK), jnp.float32)
    identity = jnp.eye(NV, dtype=jnp.float32)[:, :, None, None, None]
    return offdiag * (1.0 - identity) + identity * diagonal[:, None]


def set_ends(result, own_key, least, high):
    dims = result.shape
    spot = [jax.random.randint(jax.random.fold_in(own_key, axis), (), 0, dims[axis]) for axis in range(len(dims))]
    result = result.at[tuple(spot)].set(least)
    longest = dims.index(max(dims))
    spot[longest] = (spot[longest] + 1) % dims[longest]
    return result.at[tuple(spot)].set(high)


def levels(rng, extent, cuts, low, largest):
    def one(dim, blocks):
        steps = jax.random.uniform(jax.random.fold_in(jax.random.fold_in(rng, 6), dim), (blocks,), jnp.float32, low / len(cuts), largest / len(cuts))
        return jnp.repeat(jnp.exp(steps), extent[dim] // blocks).reshape((-1,) + (1,) * (len(extent) - dim - 1))

    level = one(*cuts[0])
    for cut in cuts[1:]:
        level = level * one(*cut)
    return level


def noise(key, shape, spread, limit, pieces=(), kind=jnp.bfloat16):
    entries = spread * jax.random.normal(key, shape, jnp.float32)
    if pieces:
        entries = entries * levels(key, shape, pieces, -0.22, 0.18)
    return jnp.clip(entries, -limit, limit).astype(kind)


def setup_inputs(seed: int = 0) -> dict:
    key_of = jax.random.split(jax.random.key(seed), 7)
    adjoint_start = noise(key_of[0], (NV, NI, NJ, NK), 0.3, 4.0, ((1, 16), (2, 2)), jnp.float32)
    source = draw_source(jax.random.fold_in(key_of[6], 71), 0)
    flow_state = draw_flow_state(jax.random.fold_in(key_of[6], 71), 0)
    precond = draw_precond(jax.random.fold_in(key_of[6], 71), 0)
    flux_jac = noise(key_of[4], (3, NV, NV), 0.3, 4.0, (), jnp.float32)
    bc_codes = set_ends(jax.random.randint(key_of[5], (NI, NJ), 0, 3), jax.random.fold_in(key_of[5], 1), 0, 2).astype(jnp.int32)
    return dict(adjoint_start=adjoint_start, source=source, flow_state=flow_state, precond=precond, flux_jac=flux_jac, bc_codes=bc_codes)


def transposed(jacobian, jump):
    return jnp.einsum('uv,u...->v...', jacobian, jump, precision=lax.Precision.HIGHEST)

def face_terms(left_side, right_side, speed_left, speed_right, jacobian):
    jump = left_side - right_side
    spectral = 0.5 * (speed_left + speed_right)
    central = 0.5 * transposed(jacobian, jump)
    upwind = 0.5 * spectral[None] * jump
    return (central + upwind, central - upwind)

def axis_term(adjoint_pad, speed_padded, jacobian, axis_dim):
    planes = adjoint_pad.shape[axis_dim] - 2
    to_left, to_right = face_terms(lax.slice_in_dim(adjoint_pad, 0, planes + 1, axis=axis_dim), lax.slice_in_dim(adjoint_pad, 1, planes + 2, axis=axis_dim), lax.slice_in_dim(speed_padded, 0, planes + 1, axis=axis_dim - 1), lax.slice_in_dim(speed_padded, 1, planes + 2, axis=axis_dim - 1), jacobian)
    return lax.slice_in_dim(to_left, 1, planes + 1, axis=axis_dim) + lax.slice_in_dim(to_right, 0, planes, axis=axis_dim)

def wall_term(adjoint, speeds, jacobian, bc_codes):
    bottom = adjoint[:, :, :, 0]
    signs = jnp.array([1.0, 1.0, 1.0, -1.0, 1.0], dtype=jnp.float32)[:, None, None]
    factor = jnp.where((bc_codes == 0)[None], signs, jnp.where((bc_codes == 2)[None], 1.0, 0.0)).astype(jnp.float32)
    return -factor * (0.5 * transposed(jacobian, bottom) + 0.25 * speeds[None, :, :, 0] * bottom)

def speeds_of(flow_state):
    density = flow_state[0]
    momentum = flow_state[1:4]
    pressure = flow_state[4]
    return jnp.sqrt(lax.optimization_barrier(jnp.sum(momentum * momentum, axis=0))) / density + jnp.sqrt(1.4 * pressure / density)

def precondition(precond, residual):
    total = precond[0] * residual[0]
    for row_index in range(1, 5):
        total = total + precond[row_index] * residual[row_index]
    return total

def adjoint_operator(adjoint, speeds, flux_jac, bc_codes):
    total = axis_term(jnp.pad(adjoint, ((0, 0), (1, 1), (0, 0), (0, 0))), jnp.pad(speeds, ((1, 1), (0, 0), (0, 0))), flux_jac[0], 1)
    total = total + axis_term(jnp.pad(adjoint, ((0, 0), (0, 0), (1, 1), (0, 0))), jnp.pad(speeds, ((0, 0), (1, 1), (0, 0))), flux_jac[1], 2)
    total = total + axis_term(jnp.pad(adjoint, ((0, 0), (0, 0), (0, 0), (1, 1))), jnp.pad(speeds, ((0, 0), (0, 0), (1, 1))), flux_jac[2], 3)
    bottom = wall_term(adjoint, speeds, flux_jac[2], bc_codes)
    return jnp.concatenate([total[..., :1] + bottom[..., None], total[..., 1:]], axis=3)

def reference(adjoint_start, source, flow_state, precond, flux_jac, bc_codes):
    speeds = speeds_of(flow_state)
    adjoint = adjoint_start
    rms_list = []
    for sweep_index in range(SWEEPS):
        residual = source - adjoint_operator(adjoint, speeds, flux_jac, bc_codes)
        rms_list.append(jnp.sqrt(jnp.sum(residual * residual) / residual.size))
        adjoint = adjoint + precondition(precond, residual)
    return (adjoint, jnp.stack(rms_list))
```

```python
import functools

import jax
import jax.numpy as jnp
from jax import lax
from jax.experimental import pallas as pl
from jax.experimental.pallas import tpu as pltpu
from jax.sharding import PartitionSpec as P

NV = 5
SUB, LANE = 8, 128
F32 = jnp.float32
VMEM = pl.BlockSpec(memory_space=pltpu.VMEM)
SMEM = pl.BlockSpec(memory_space=pltpu.SMEM)


def shape(*dims):
    return jax.ShapeDtypeStruct(dims, F32)


def cost(flops, transcendentals, bytes_accessed):
    return pl.CostEstimate(
        flops=int(flops), transcendentals=int(transcendentals), bytes_accessed=int(bytes_accessed)
    )


def quarter_speed(rho, m1, m2, m3, p):
    momentum = jnp.sqrt(m1 * m1 + m2 * m2 + m3 * m3)
    return 0.25 * (momentum / rho + jnp.sqrt(1.4 * p / rho))


def odd(axis):
    return lax.rem(lax.axis_index(axis), 2) == 1


def stream_faces(v, fa, fb):
    planes = v.shape[1]
    is_odd = odd("stream")
    plane_a = jnp.where(is_odd, 0, planes - 1)
    plane_b = jnp.where(is_odd, planes - 1, 0)
    for c in range(NV):
        fa[c] = v[c, plane_a]
        fb[c] = v[c, plane_b]
    return plane_a, plane_b


def span_rows(v, c, first, last, out_refs):
    is_odd = odd("span")
    planes = v.shape[1]
    for i in range(planes):
        head = v[c, i, first : first + 1, :]
        tail = v[c, i, last : last + 1, :]
        out_refs[0][c, i] = jnp.where(is_odd, head, tail)
        if len(out_refs) > 1:
            out_refs[1][c, i] = jnp.where(is_odd, tail, head)


def pack_kernel(n_span, v, flow, fa, fb, *rest):
    spans, rows = rest[:n_span], rest[n_span:]
    plane_a, plane_b = stream_faces(v, fa, fb)
    for ref, plane in ((fa, plane_a), (fb, plane_b)):
        ref[NV] = quarter_speed(*[flow[c, plane] for c in range(NV)])
    last = v.shape[2] - 1
    for c in range(NV):
        span_rows(v, c, 0, last, spans)
        span_rows(flow, c, 0, last, rows)
    for ref, row in zip(spans, rows):
        ref[NV] = quarter_speed(*[row[c] for c in range(NV)])


def sweep_plane(i, v, prev, nxt, g, gprev, gnxt, tops, bottoms, src, pre, jac, wall, out, ssq):
    rows_n, lanes_n = v.shape[2] // SUB, v.shape[3] // LANE
    lane = lax.broadcasted_iota(jnp.int32, (SUB, LANE), 1)
    row = lax.broadcasted_iota(jnp.int32, (SUB, LANE), 0)
    first_lane, last_lane = lane == 0, lane == LANE - 1
    first_row, last_row = row == 0, row == SUB - 1
    zero = jnp.zeros((SUB, LANE), F32)

    def at(jb, kb):
        return pl.ds(jb * SUB, SUB), pl.ds(kb * LANE, LANE)

    def neighbours(get, get_top, get_bottom, jb, kb):
        own = get(jb, kb)
        up = pltpu.roll(own, 1, 0)
        before_row = get_top(kb) if jb == 0 else pltpu.roll(get(jb - 1, kb), 1, 0)
        up = jnp.where(first_row, before_row, up)
        down = pltpu.roll(own, SUB - 1, 0)
        after_row = get_bottom(kb) if jb == rows_n - 1 else pltpu.roll(get(jb + 1, kb), SUB - 1, 0)
        down = jnp.where(last_row, after_row, down)
        left = pltpu.roll(own, 1, 1)
        left = jnp.where(first_lane, zero if kb == 0 else pltpu.roll(get(jb, kb - 1), 1, 1), left)
        right = pltpu.roll(own, LANE - 1, 1)
        right = jnp.where(
            last_lane, zero if kb == lanes_n - 1 else pltpu.roll(get(jb, kb + 1), LANE - 1, 1), right
        )
        return own, up, down, left, right

    total = ssq
    for jb in range(rows_n):
        for kb in range(lanes_n):
            sl = at(jb, kb)
            gs, gu, gd, gl, gr = neighbours(
                lambda a, b: g[(i, *at(a, b))],
                lambda b: tops(NV, b),
                lambda b: bottoms(NV, b),
                jb,
                kb,
            )
            coefs = [gs + gprev(*sl), gs + gnxt(*sl), gs + gu, gs + gd, gs + gl, gs + gr]
            diag = ((coefs[0] + coefs[1]) + (coefs[2] + coefs[3])) + (coefs[4] + coefs[5])
            diffs, owns, res = [], [], []
            for c in range(NV):
                own, up, down, left, right = neighbours(
                    lambda a, b, c=c: v[(c, i, *at(a, b))],
                    functools.partial(tops, c),
                    functools.partial(bottoms, c),
                    jb,
                    kb,
                )
                before, after = prev(c, *sl), nxt(c, *sl)
                diffs.append((before - after, up - down, left - right))
                owns.append(own)
                pulls = (
                    (coefs[0] * before + coefs[1] * after)
                    + (coefs[2] * up + coefs[3] * down)
                ) + (coefs[4] * left + coefs[5] * right)
                res.append(src[(c, i, *sl)] - (diag * own - pulls))
            for c in range(NV):
                r = res[c]
                for d in range(3):
                    for u in range(NV):
                        r = r - jac[d, u, c] * diffs[u][d]
                res[c] = r
            if kb == 0:
                code = wall(jb)
                on_wall = first_lane & (code != 1)
                for c in range(NV):
                    t = gs * owns[c]
                    for u in range(NV):
                        t = t + jac[2, u, c] * owns[u]
                    if c == 3:
                        t = jnp.where(code == 0, -t, t)
                    res[c] = res[c] + jnp.where(on_wall, t, zero)
            for c in range(NV):
                total = total + res[c] * res[c]
            for c in range(NV):
                a = owns[c]
                for u in range(NV):
                    a = a + pre[(u, c, i, *sl)] * res[u]
                out[(c, i, *sl)] = a
    return total


def spread_codes(bc, codes):
    planes, columns = bc.shape
    eye = lax.broadcasted_iota(jnp.int32, (columns, columns), 0) == lax.broadcasted_iota(
        jnp.int32, (columns, columns), 1
    )
    for i in range(planes):
        own = jnp.broadcast_to(bc[i : i + 1, :].astype(F32), (columns, columns))
        column = jnp.sum(jnp.where(eye, own, 0.0), axis=1, keepdims=True)
        codes[i] = jnp.broadcast_to(column, (columns, LANE))


def sweep_kernel(first, n_span, *refs):
    refs = list(refs)
    v = refs.pop(0)
    src = refs.pop(0)
    pre = refs.pop(0)
    jac_in = refs.pop(0)
    bc = refs.pop(0)
    speed_in = refs.pop(0)
    ha, hb = refs.pop(0), refs.pop(0)
    spans = [refs.pop(0) for _ in range(n_span)]
    if not first:
        gha, ghb = refs.pop(0), refs.pop(0)
        gspans = [refs.pop(0) for _ in range(n_span)]
    else:
        gha, ghb, gspans = ha, hb, spans
    out, ssq_out = refs.pop(0), refs.pop(0)
    if first:
        g = refs.pop(0)
        fa, fb = refs.pop(0), refs.pop(0)
        span_out = [refs.pop(0) for _ in range(n_span)]
    else:
        g = speed_in
    halves, codes = refs
    planes = v.shape[1]
    spread_codes(bc, codes)

    for d in range(3):
        for u in range(NV):
            for c in range(NV):
                halves[d, u, c] = 0.5 * jac_in[d, u, c]
    if first:

        def speed_plane(i, carry):
            g[i] = quarter_speed(*[speed_in[c, i] for c in range(NV)])
            return carry

        lax.fori_loop(0, planes, speed_plane, 0)

    stream_odd, span_odd = odd("stream"), odd("span")

    def pick(is_odd, pair, even_ref, idx):
        other = 1 - even_ref
        if len(pair) == 1:
            keep = is_odd if even_ref == 1 else jnp.logical_not(is_odd)
            return jnp.where(keep, pair[0][idx], 0.0)
        return jnp.where(is_odd, pair[other][idx], pair[even_ref][idx])

    def low_halo(c, *sl):
        pair = (gha, ghb) if c == NV else (ha, hb)
        return pick(stream_odd, pair, 1, (c, *sl))

    def high_halo(c, *sl):
        pair = (gha, ghb) if c == NV else (ha, hb)
        return pick(stream_odd, pair, 0, (c, *sl))

    def rows_of(even_ref, i):
        def get(c, kb):
            pair = gspans if c == NV else spans
            one = pick(span_odd, pair, even_ref, (c, i, slice(None), pl.ds(kb * LANE, LANE)))
            return jnp.broadcast_to(one, (SUB, LANE))

        return get

    def plane(i, prev, nxt, gprev, gnxt, ssq):
        return sweep_plane(
            i, v, prev, nxt, g, gprev, gnxt, rows_of(1, i), rows_of(0, i), src, pre, halves,
            lambda jb: codes[i, pl.ds(jb * SUB, SUB), :],
            out, ssq,
        )

    def inner(i, ssq):
        return plane(
            i,
            lambda c, *sl: v[(c, i - 1, *sl)],
            lambda c, *sl: v[(c, i + 1, *sl)],
            lambda *sl: g[(i - 1, *sl)],
            lambda *sl: g[(i + 1, *sl)],
            ssq,
        )

    ssq = jnp.zeros((SUB, LANE), F32)
    ssq = lax.fori_loop(1, planes - 1, inner, ssq)
    ssq = plane(
        0, low_halo, lambda c, *sl: v[(c, 1, *sl)],
        lambda *sl: low_halo(NV, *sl), lambda *sl: g[(1, *sl)], ssq,
    )
    ssq = plane(
        planes - 1, lambda c, *sl: v[(c, planes - 2, *sl)], high_halo,
        lambda *sl: g[(planes - 2, *sl)], lambda *sl: high_halo(NV, *sl), ssq,
    )
    ssq_out[...] = ssq
    if first:
        stream_faces(out, fa, fb)
        for c in range(NV):
            span_rows(out, c, 0, v.shape[2] - 1, span_out)


def pairs(count, offset):
    both = []
    for i in range(offset, count - 1, 2):
        both += [(i, i + 1), (i + 1, i)]
    return both


def exchange(faces, axis):
    count = lax.axis_size(axis)
    return [lax.ppermute(face, axis, pairs(count, k)) for k, face in enumerate(faces)]


def all_sum(value):
    for axis in ("span", "stream"):
        count = lax.axis_size(axis)
        if count & (count - 1):
            value = lax.psum(value, axis)
            continue
        step = 1
        while step < count:
            value = value + lax.ppermute(value, axis, [(i, i ^ step) for i in range(count)])
            step *= 2
    return value


def finish_kernel(a, b, out):
    lane = lax.broadcasted_iota(jnp.int32, (SUB, LANE), 1)
    out[...] = jnp.where(lane == 0, jnp.sum(a[...]), jnp.where(lane == 1, jnp.sum(b[...]), 0.0))


def per_device(adjoint_start, source, flow_state, precond, flux_jac, bc_codes):
    _, planes, rows, lanes = adjoint_start.shape
    n_stream, n_span_all = lax.axis_size("stream"), lax.axis_size("span")
    n_span = 1 if n_span_all <= 2 else 2
    cells = planes * rows * lanes
    cells_all = float(NV * cells * n_stream * n_span_all)
    scratch = [pltpu.SMEM((3, NV, NV), F32), pltpu.VMEM((planes, rows, LANE), F32)]

    faces = pl.pallas_call(
        functools.partial(pack_kernel, n_span),
        out_shape=[shape(NV + 1, rows, lanes)] * 2 + [shape(NV + 1, planes, 1, lanes)] * n_span,
        in_specs=[VMEM] * 2,
        out_specs=[VMEM] * (2 + n_span),
        scratch_shapes=[pltpu.VMEM((NV, planes, 1, lanes), F32)] * n_span,
        cost_estimate=cost(cells, 0, 8 * cells),
        name="pack",
    )(adjoint_start, flow_state)
    stream0 = exchange(faces[:2], "stream")
    span0 = exchange(faces[2:], "span")

    outs = pl.pallas_call(
        functools.partial(sweep_kernel, True, n_span),
        out_shape=[shape(NV, planes, rows, lanes), shape(SUB, LANE), shape(planes, rows, lanes)]
        + [shape(NV, rows, lanes)] * 2
        + [shape(NV, planes, 1, lanes)] * n_span,
        in_specs=[VMEM] * 3 + [SMEM] + [VMEM] * (4 + n_span),
        out_specs=[VMEM] * (5 + n_span),
        scratch_shapes=scratch,
        cost_estimate=cost(350 * cells, 4 * cells, 42 * 4 * cells),
        name="sweep_first",
    )(adjoint_start, source, precond, flux_jac, bc_codes, flow_state, *stream0, *span0)
    adjoint, ssq0, quarter = outs[:3]
    stream1 = exchange(outs[3:5], "stream")
    span1 = exchange(outs[5:], "span")

    adjoint, ssq1 = pl.pallas_call(
        functools.partial(sweep_kernel, False, n_span),
        out_shape=[shape(NV, planes, rows, lanes), shape(SUB, LANE)],
        in_specs=[VMEM] * 3 + [SMEM] + [VMEM] * (6 + 2 * n_span),
        out_specs=[VMEM] * 2,
        scratch_shapes=scratch,
        cost_estimate=cost(350 * cells, 0, 42 * 4 * cells),
        name="sweep_second",
    )(adjoint, source, precond, flux_jac, bc_codes, quarter, *stream1, *span1, *stream0, *span0)

    sums = pl.pallas_call(
        finish_kernel, out_shape=shape(SUB, LANE), in_specs=[VMEM] * 2, out_specs=VMEM, name="sums"
    )(ssq0, ssq1)
    residual_rms = jnp.sqrt(all_sum(sums)[0, :2] / cells_all)
    return (adjoint, residual_rms)


def solution(mesh):
    in_specs = (
        P(None, "stream", "span", None),
        P(None, "stream", "span", None),
        P(None, "stream", "span", None),
        P(None, None, "stream", "span", None),
        P(),
        P("stream", "span"),
    )
    out_specs = (P(None, "stream", "span", None), P())
    return jax.shard_map(
        per_device, mesh=mesh, in_specs=in_specs, out_specs=out_specs, check_vma=False
    )
```

```python
import functools

import jax
import jax.numpy as jnp
from jax import lax
from jax.experimental import pallas as pl
from jax.experimental.pallas import tpu as pltpu
from jax.sharding import PartitionSpec as P

NV = 5
SUB, LANE = 8, 128
F32 = jnp.float32
VMEM = pl.BlockSpec(memory_space=pltpu.VMEM)
HBM = pl.BlockSpec(memory_space=pltpu.HBM)
SMEM = pl.BlockSpec(memory_space=pltpu.SMEM)


def shape(*dims):
    return pltpu.VMEM(dims, F32)


def hold(*arrays, space=pltpu.VMEM):
    return [pltpu.with_memory_space_constraint(a, space) for a in arrays]


def params():
    return pltpu.CompilerParams(vmem_limit_bytes=4 << 20)


def cost(flops, transcendentals, bytes_accessed):
    return pl.CostEstimate(
        flops=int(flops), transcendentals=int(transcendentals), bytes_accessed=int(bytes_accessed)
    )


def quarter_speed(rho, m1, m2, m3, p):
    momentum = jnp.sqrt(m1 * m1 + m2 * m2 + m3 * m3)
    return 0.25 * (momentum / rho + jnp.sqrt(1.4 * p / rho))


def odd(axis):
    return lax.rem(lax.axis_index(axis), 2) == 1


def stream_faces(v, fa, fb):
    planes = v.shape[1]
    is_odd = odd("stream")
    plane_a = jnp.where(is_odd, 0, planes - 1)
    plane_b = jnp.where(is_odd, planes - 1, 0)
    for c in range(NV):
        fa[c] = v[c, plane_a]
        fb[c] = v[c, plane_b]
    return plane_a, plane_b


def span_rows(v, c, first, last, out_refs):
    is_odd = odd("span")
    planes = v.shape[1]
    for i in range(planes):
        head = v[c, i, first : first + 1, :]
        tail = v[c, i, last : last + 1, :]
        out_refs[0][c, i] = jnp.where(is_odd, head, tail)
        if len(out_refs) > 1:
            out_refs[1][c, i] = jnp.where(is_odd, tail, head)


def pack_kernel(n_span, v_hbm, flow_hbm, v, flow, fa, fb, *rest):
    spans, rows, sem = rest[:n_span], rest[n_span:-1], rest[-1]
    copies = [
        pltpu.make_async_copy(src, dst, sem.at[k])
        for k, (src, dst) in enumerate(((flow_hbm, flow), (v_hbm, v)))
    ]
    for copy in copies:
        copy.start()
    for copy in copies:
        copy.wait()
    plane_a, plane_b = stream_faces(v, fa, fb)
    for ref, plane in ((fa, plane_a), (fb, plane_b)):
        ref[NV] = quarter_speed(*[flow[c, plane] for c in range(NV)])
    last = v.shape[2] - 1
    for c in range(NV):
        span_rows(v, c, 0, last, spans)
        span_rows(flow, c, 0, last, rows)
    for ref, row in zip(spans, rows):
        ref[NV] = quarter_speed(*[row[c] for c in range(NV)])


def sweep_plane(i, v, prev, nxt, g, gprev, gnxt, tops, bottoms, src, pre, jac, wall, out, ssq):
    rows_n, lanes_n = v.shape[2] // SUB, v.shape[3] // LANE
    lane = lax.broadcasted_iota(jnp.int32, (SUB, LANE), 1)
    row = lax.broadcasted_iota(jnp.int32, (SUB, LANE), 0)
    first_lane, last_lane = lane == 0, lane == LANE - 1
    first_row, last_row = row == 0, row == SUB - 1
    zero = jnp.zeros((SUB, LANE), F32)

    def at(jb, kb):
        return pl.ds(jb * SUB, SUB), pl.ds(kb * LANE, LANE)

    def neighbours(get, get_top, get_bottom, jb, kb):
        own = get(jb, kb)
        up = pltpu.roll(own, 1, 0)
        before_row = get_top(kb) if jb == 0 else pltpu.roll(get(jb - 1, kb), 1, 0)
        up = jnp.where(first_row, before_row, up)
        down = pltpu.roll(own, SUB - 1, 0)
        after_row = get_bottom(kb) if jb == rows_n - 1 else pltpu.roll(get(jb + 1, kb), SUB - 1, 0)
        down = jnp.where(last_row, after_row, down)
        left = pltpu.roll(own, 1, 1)
        left = jnp.where(first_lane, zero if kb == 0 else pltpu.roll(get(jb, kb - 1), 1, 1), left)
        right = pltpu.roll(own, LANE - 1, 1)
        right = jnp.where(
            last_lane, zero if kb == lanes_n - 1 else pltpu.roll(get(jb, kb + 1), LANE - 1, 1), right
        )
        return own, up, down, left, right

    total = ssq
    for jb in range(rows_n):
        for kb in range(lanes_n):
            sl = at(jb, kb)
            gs, gu, gd, gl, gr = neighbours(
                lambda a, b: g[(i, *at(a, b))],
                lambda b: tops(NV, b),
                lambda b: bottoms(NV, b),
                jb,
                kb,
            )
            coefs = [gs + gprev(*sl), gs + gnxt(*sl), gs + gu, gs + gd, gs + gl, gs + gr]
            diag = ((coefs[0] + coefs[1]) + (coefs[2] + coefs[3])) + (coefs[4] + coefs[5])
            diffs, owns, res = [], [], []
            for c in range(NV):
                own, up, down, left, right = neighbours(
                    lambda a, b, c=c: v[(c, i, *at(a, b))],
                    functools.partial(tops, c),
                    functools.partial(bottoms, c),
                    jb,
                    kb,
                )
                before, after = prev(c, *sl), nxt(c, *sl)
                diffs.append((before - after, up - down, left - right))
                owns.append(own)
                pulls = (
                    (coefs[0] * before + coefs[1] * after)
                    + (coefs[2] * up + coefs[3] * down)
                ) + (coefs[4] * left + coefs[5] * right)
                res.append(src[(c, i, *sl)] - (diag * own - pulls))
            for c in range(NV):
                r = res[c]
                for d in range(3):
                    for u in range(NV):
                        r = r - jac[d, u, c] * diffs[u][d]
                res[c] = r
            if kb == 0:
                code = wall(jb)
                on_wall = first_lane & (code != 1)
                for c in range(NV):
                    t = gs * owns[c]
                    for u in range(NV):
                        t = t + jac[2, u, c] * owns[u]
                    if c == 3:
                        t = jnp.where(code == 0, -t, t)
                    res[c] = res[c] + jnp.where(on_wall, t, zero)
            for c in range(NV):
                total = total + res[c] * res[c]
            for c in range(NV):
                a = owns[c]
                for u in range(NV):
                    a = a + pre[(u, c, i, *sl)] * res[u]
                out[(c, i, *sl)] = a
    return total


def spread_codes(bc, codes):
    planes, columns = bc.shape
    eye = lax.broadcasted_iota(jnp.int32, (columns, columns), 0) == lax.broadcasted_iota(
        jnp.int32, (columns, columns), 1
    )
    for i in range(planes):
        own = jnp.broadcast_to(bc[i : i + 1, :].astype(F32), (columns, columns))
        column = jnp.sum(jnp.where(eye, own, 0.0), axis=1, keepdims=True)
        codes[i] = jnp.broadcast_to(column, (columns, LANE))


def pick(is_odd, pair, even_ref, idx):
    if len(pair) == 1:
        keep = is_odd if even_ref == 1 else jnp.logical_not(is_odd)
        return jnp.where(keep, pair[0][idx], 0.0)
    return jnp.where(is_odd, pair[1 - even_ref][idx], pair[even_ref][idx])


def make_plane(v, g, src, pre, jac, codes, out, streams, g_streams, spans, g_spans):
    planes = v.shape[1]
    stream_odd, span_odd = odd("stream"), odd("span")

    def halo(even_ref):
        return lambda c, *sl: pick(
            stream_odd, g_streams if c == NV else streams, even_ref, (c, *sl)
        )

    def rows_of(even_ref, i):
        def get(c, kb):
            pair = g_spans if c == NV else spans
            one = pick(span_odd, pair, even_ref, (c, i, slice(None), pl.ds(kb * LANE, LANE)))
            return jnp.broadcast_to(one, (SUB, LANE))

        return get

    def plane(i, ssq):
        first = isinstance(i, int) and i == 0
        last = isinstance(i, int) and i == planes - 1
        low, high = halo(1), halo(0)
        return sweep_plane(
            i,
            v,
            low if first else lambda c, *sl: v[(c, i - 1, *sl)],
            high if last else lambda c, *sl: v[(c, i + 1, *sl)],
            g,
            (lambda *sl: low(NV, *sl)) if first else lambda *sl: g[(i - 1, *sl)],
            (lambda *sl: high(NV, *sl)) if last else lambda *sl: g[(i + 1, *sl)],
            rows_of(1, i),
            rows_of(0, i),
            src,
            pre,
            jac,
            lambda jb: codes[i, pl.ds(jb * SUB, SUB), :],
            out,
            ssq,
        )

    return plane


def no_sum():
    return jnp.zeros((SUB, LANE), F32)


def first_inner(n_span, v, flow, src_hbm, pre_hbm, jac, bc, *refs):
    spans = refs[:n_span]
    out, g, src, pre, codes, ssq_out, sem = refs[n_span:]
    planes = v.shape[1]

    def loads(i):
        return (
            pltpu.make_async_copy(src_hbm.at[:, i], src.at[:, i], sem.at[0, i]),
            pltpu.make_async_copy(pre_hbm.at[:, :, i], pre.at[:, :, i], sem.at[1, i]),
        )

    for i in [*range(1, planes - 1), 0, planes - 1]:
        for load in loads(i):
            load.start()
    spread_codes(bc, codes)

    def speed_plane(i, carry):
        g[i] = quarter_speed(*[flow[c, i] for c in range(NV)])
        return carry

    lax.fori_loop(0, planes, speed_plane, 0)
    plane = make_plane(v, g, src, pre, jac, codes, out, (), (), spans, spans)

    def inner(i, ssq):
        for load in loads(i):
            load.wait()
        return plane(i, ssq)

    ssq_out[...] = lax.fori_loop(1, planes - 1, inner, no_sum())
    for i in (0, planes - 1):
        for load in loads(i):
            load.wait()


def first_edge(n_span, v, g, src, pre, jac, codes, ssq_in, out_in, ha, hb, *refs):
    spans = refs[:n_span]
    out, ssq_out, fa, fb = refs[n_span : n_span + 4]
    span_out = refs[n_span + 4 :]
    planes = v.shape[1]
    plane = make_plane(v, g, src, pre, jac, codes, out, (ha, hb), (ha, hb), spans, spans)
    ssq_out[...] = plane(planes - 1, plane(0, ssq_in[...]))
    stream_faces(out, fa, fb)
    for c in range(NV):
        span_rows(out, c, 0, v.shape[2] - 1, span_out)


def second_inner(n_span, v, g, src, pre, jac, codes, *refs):
    spans, g_spans = refs[:n_span], refs[n_span : 2 * n_span]
    out_hbm, ssq_out, out, sem = refs[2 * n_span :]
    planes = v.shape[1]
    plane = make_plane(v, g, src, pre, jac, codes, out, (), (), spans, g_spans)

    def store(i):
        return pltpu.make_async_copy(out.at[:, i], out_hbm.at[:, i], sem.at[i])

    def inner(i, ssq):
        ssq = plane(i, ssq)
        store(i).start()
        return ssq

    ssq_out[...] = lax.fori_loop(1, planes - 1, inner, no_sum())

    def finish(i, carry):
        store(i).wait()
        return carry

    lax.fori_loop(1, planes - 1, finish, 0)


def second_edge(n_span, v, g, src, pre, jac, codes, ssq_before, ssq_in, out_in, *refs):
    streams, g_streams = refs[:2], refs[2:4]
    spans, g_spans = refs[4 : 4 + n_span], refs[4 + n_span : 4 + 2 * n_span]
    out_hbm, sums, out, sem = refs[4 + 2 * n_span :]
    planes = v.shape[1]
    plane = make_plane(v, g, src, pre, jac, codes, out, streams, g_streams, spans, g_spans)
    ssq = ssq_in[...]
    stores = []
    for k, i in enumerate((0, planes - 1)):
        ssq = plane(i, ssq)
        stores.append(pltpu.make_async_copy(out.at[:, i], out_hbm.at[:, i], sem.at[k]))
        stores[-1].start()
    lane = lax.broadcasted_iota(jnp.int32, sums.shape, 1)
    before, now = jnp.sum(ssq_before[...]), jnp.sum(ssq)
    sums[...] = jnp.where(lane == 0, before, jnp.where(lane == 1, now, 0.0))
    for store in stores:
        store.wait()


def pairs(count, offset):
    both = []
    for i in range(offset, count - 1, 2):
        both += [(i, i + 1), (i + 1, i)]
    return both


def exchange(faces, axis):
    count = lax.axis_size(axis)
    return [lax.ppermute(face, axis, pairs(count, k)) for k, face in enumerate(faces)]


def per_device(adjoint_start, source, flow_state, precond, flux_jac, bc_codes):
    _, planes, rows, lanes = adjoint_start.shape
    n_stream, n_span_all = lax.axis_size("stream"), lax.axis_size("span")
    n_devices = n_stream * n_span_all
    n_span = 1 if n_span_all <= 2 else 2
    cells = planes * rows * lanes
    field = shape(NV, planes, rows, lanes)
    tile = shape(SUB, LANE)
    dma = pltpu.SemaphoreType.DMA
    jac = 0.5 * flux_jac
    inner_cost = cost(3000 * cells, 4 * cells, 42 * 4 * cells)
    edge_cost = cost(100 * cells, 0, 42 * cells)

    v, flow, *faces = pl.pallas_call(
        functools.partial(pack_kernel, n_span),
        out_shape=[field, field]
        + [shape(NV + 1, rows, lanes)] * 2
        + [shape(NV + 1, planes, 1, lanes)] * n_span,
        in_specs=[HBM] * 2,
        out_specs=[VMEM] * (4 + n_span),
        scratch_shapes=[pltpu.VMEM((NV, planes, 1, lanes), F32)] * n_span + [dma((2,))],
        cost_estimate=cost(cells, 0, 8 * cells),
        compiler_params=params(),
        name="pack",
    )(*hold(adjoint_start, flow_state, space=pltpu.HBM))
    streams = exchange(faces[:2], "stream")
    spans = exchange(faces[2:], "span")

    adjoint, g, src, pre, codes, ssq = pl.pallas_call(
        functools.partial(first_inner, n_span),
        out_shape=[
            field, shape(planes, rows, lanes), field, shape(NV, NV, planes, rows, lanes),
            shape(planes, rows, LANE), tile,
        ],
        in_specs=[VMEM] * 2 + [HBM] * 2 + [SMEM] + [VMEM] * (1 + n_span),
        out_specs=[VMEM] * 6,
        scratch_shapes=[dma((2, planes))],
        cost_estimate=inner_cost,
        compiler_params=params(),
        name="first_inner",
    )(*hold(v, flow), *hold(source, precond, space=pltpu.HBM), jac, *hold(bc_codes, *spans))

    adjoint, ssq_first, *faces = pl.pallas_call(
        functools.partial(first_edge, n_span),
        out_shape=[field, tile]
        + [shape(NV, rows, lanes)] * 2
        + [shape(NV, planes, 1, lanes)] * n_span,
        in_specs=[VMEM] * 4 + [SMEM] + [VMEM] * (5 + n_span),
        out_specs=[VMEM] * (4 + n_span),
        input_output_aliases={7: 0},
        cost_estimate=edge_cost,
        compiler_params=params(),
        name="first_edge",
    )(*hold(v, g, src, pre), jac, *hold(codes, ssq, adjoint, *streams, *spans))
    streams_next = exchange(faces[:2], "stream")
    spans_next = exchange(faces[2:], "span")

    result, ssq = pl.pallas_call(
        functools.partial(second_inner, n_span),
        out_shape=[pltpu.HBM(adjoint_start.shape, F32), tile],
        in_specs=[VMEM] * 4 + [SMEM] + [VMEM] * (1 + 2 * n_span),
        out_specs=[HBM, VMEM],
        scratch_shapes=[field, dma((planes,))],
        cost_estimate=inner_cost,
        compiler_params=params(),
        name="second_inner",
    )(*hold(adjoint, g, src, pre), jac, *hold(codes, *spans_next, *spans))

    result, sums = pl.pallas_call(
        functools.partial(second_edge, n_span),
        out_shape=[pltpu.HBM(adjoint_start.shape, F32), shape(n_devices, LANE)],
        in_specs=[VMEM] * 4 + [SMEM] + [VMEM] * 3 + [HBM] + [VMEM] * (4 + 2 * n_span),
        out_specs=[HBM, VMEM],
        scratch_shapes=[field, dma((2,))],
        input_output_aliases={8: 0},
        cost_estimate=edge_cost,
        compiler_params=params(),
        name="second_edge",
    )(
        *hold(adjoint, g, src, pre), jac, *hold(codes, ssq_first, ssq), *hold(result, space=pltpu.HBM),
        *hold(*streams_next, *streams, *spans_next, *spans),
    )
    sums = lax.all_to_all(sums, ("stream", "span"), 0, 0, tiled=True)
    cells_all = float(NV * cells * n_devices)
    return (result, jnp.sqrt(jnp.sum(sums, axis=0)[:2] / cells_all))


def solution(mesh):
    in_specs = (
        P(None, "stream", "span", None),
        P(None, "stream", "span", None),
        P(None, "stream", "span", None),
        P(None, None, "stream", "span", None),
        P(),
        P("stream", "span"),
    )
    out_specs = (P(None, "stream", "span", None), P())
    return jax.shard_map(
        per_device, mesh=mesh, in_specs=in_specs, out_specs=out_specs, check_vma=False
    )
```

```python
import functools

import jax
import jax.numpy as jnp
from jax import lax
from jax.experimental import pallas as pl
from jax.experimental.pallas import tpu as pltpu
from jax.sharding import PartitionSpec as P


NV = 5
SUB, LANE = 8, 128
F32 = jnp.float32
VMEM = pl.BlockSpec(memory_space=pltpu.VMEM)
HBM = pl.BlockSpec(memory_space=pltpu.HBM)


def shape(*dims):
    return pltpu.VMEM(dims, F32)


def hold(*arrays, space=pltpu.VMEM):
    return [pltpu.with_memory_space_constraint(a, space) for a in arrays]


def params():
    return pltpu.CompilerParams(vmem_limit_bytes=4 << 20)


def cost(flops, transcendentals, bytes_accessed):
    return pl.CostEstimate(
        flops=int(flops), transcendentals=int(transcendentals), bytes_accessed=int(bytes_accessed)
    )


def quarter_speed(rho, m1, m2, m3, p):
    momentum = jnp.sqrt(m1 * m1 + m2 * m2 + m3 * m3)
    return 0.25 * (momentum / rho + jnp.sqrt(1.4 * p / rho))


def odd(axis):
    return lax.rem(lax.axis_index(axis), 2) == 1


def face_planes(planes):
    is_odd = odd("stream")
    return jnp.where(is_odd, 0, planes - 1), jnp.where(is_odd, planes - 1, 0)


def span_rows(field, c, i, out_refs, k):
    is_odd = odd("span")
    last = field.shape[2] - 1
    head = field[c, i, 0:1, :]
    tail = field[c, i, last : last + 1, :]
    out_refs[0][c, k] = jnp.where(is_odd, head, tail)
    if len(out_refs) > 1:
        out_refs[1][c, k] = jnp.where(is_odd, tail, head)


def pack_kernel(n_span, v_hbm, flow_hbm, v, flow, fa, fb, *rest):
    spans, rows, sem = rest[:n_span], rest[n_span:-1], rest[-1]
    planes = v.shape[1]

    def loads(at, k):
        return [
            pltpu.make_async_copy(src.at[:, at], dst.at[:, at], sem.at[n, k])
            for n, (src, dst) in enumerate(((flow_hbm, flow), (v_hbm, v)))
        ]

    ends = face_planes(planes)
    groups = [loads(ends[0], 0), loads(ends[1], 1), loads(pl.ds(1, planes - 2), 2)]
    for group in groups:
        for load in group:
            load.start()
    for group, face, plane in zip(groups, (fa, fb), ends):
        for load in group:
            load.wait()
        face[NV] = quarter_speed(*[flow[c, plane] for c in range(NV)])
        for c in range(NV):
            face[c] = v[c, plane]
    for load in groups[2]:
        load.wait()
    for c in range(NV):
        for i in range(planes):
            span_rows(v, c, i, spans, i)
            span_rows(flow, c, i, rows, i)
    for ref, row in zip(spans, rows):
        ref[NV] = quarter_speed(*[row[c] for c in range(NV)])


def sweep_plane(i, v, prev, nxt, sign, g, gprev, gnxt, tops, bottoms, src, pre, jac, wall, put, ssq):
    rows_n, lanes_n = v.shape[2] // SUB, v.shape[3] // LANE
    lane = lax.broadcasted_iota(jnp.int32, (SUB, LANE), 1)
    row = lax.broadcasted_iota(jnp.int32, (SUB, LANE), 0)
    first_lane, last_lane = lane == 0, lane == LANE - 1
    first_row, last_row = row == 0, row == SUB - 1
    zero = jnp.zeros((SUB, LANE), F32)

    def at(jb, kb):
        return pl.ds(jb * SUB, SUB), pl.ds(kb * LANE, LANE)

    def shifts(get):
        @functools.cache
        def turned(jb, kb, shift, axis):
            return pltpu.roll(tile(jb, kb), shift % (SUB, LANE)[axis], axis)

        @functools.cache
        def tile(jb, kb):
            return get(*at(jb, kb))

        def shifted(top, bottom, jb, kb):
            before = top(kb) if jb == 0 else turned(jb - 1, kb, 1, 0)
            after = bottom(kb) if jb == rows_n - 1 else turned(jb + 1, kb, -1, 0)
            low = zero if kb == 0 else turned(jb, kb - 1, 1, 1)
            high = zero if kb == lanes_n - 1 else turned(jb, kb + 1, -1, 1)
            return (
                tile(jb, kb),
                jnp.where(first_row, before, turned(jb, kb, 1, 0)),
                jnp.where(last_row, after, turned(jb, kb, -1, 0)),
                jnp.where(first_lane, low, turned(jb, kb, 1, 1)),
                jnp.where(last_lane, high, turned(jb, kb, -1, 1)),
            )

        return shifted

    g_shift = shifts(lambda *sl: g[(i, *sl)])
    v_shift = [shifts(lambda *sl, c=c: v[(c, i, *sl)]) for c in range(NV)]
    total = ssq
    for kb in range(lanes_n):
        for jb in range(rows_n):
            sl = at(jb, kb)
            gs, gu, gd, gl, gr = g_shift(
                functools.partial(tops, NV), functools.partial(bottoms, NV), jb, kb
            )
            coefs = [gs + gprev(*sl), gs + gnxt(*sl), gs + gu, gs + gd, gs + gl, gs + gr]
            diag = ((coefs[0] + coefs[1]) + (coefs[2] + coefs[3])) + (coefs[4] + coefs[5])
            diffs, owns, res = [], [], []
            for c in range(NV):
                own, up, down, left, right = v_shift[c](
                    functools.partial(tops, c), functools.partial(bottoms, c), jb, kb
                )
                before, after = prev(c, *sl), nxt(c, *sl)
                across = before - after if sign is None else sign * (before - after)
                diffs.append((across, up - down, left - right))
                owns.append(own)
                pulls = (
                    (coefs[0] * before + coefs[1] * after)
                    + (coefs[2] * up + coefs[3] * down)
                ) + (coefs[4] * left + coefs[5] * right)
                res.append(src[(c, i, *sl)] - (diag * own - pulls))
            for c in range(NV):
                r = res[c]
                for d in range(3):
                    for u in range(NV):
                        r = r - jac[(d * NV + u) * NV + c] * diffs[u][d]
                res[c] = r
            if kb == 0:
                code = wall(jb)
                on_wall = first_lane & (code != 1)
                for c in range(NV):
                    t = gs * owns[c]
                    for u in range(NV):
                        t = t + jac[(2 * NV + u) * NV + c] * owns[u]
                    if c == 3:
                        t = jnp.where(code == 0, -t, t)
                    res[c] = res[c] + jnp.where(on_wall, t, zero)
            for c in range(NV):
                total = total + res[c] * res[c]
            for c in range(NV):
                a = owns[c]
                for u in range(NV):
                    a = a + pre[(u, c, i, *sl)] * res[u]
                put(c, sl, a)
    return total


def spread_codes(bc, codes):
    planes, columns = bc.shape
    eye = lax.broadcasted_iota(jnp.int32, (columns, columns), 0) == lax.broadcasted_iota(
        jnp.int32, (columns, columns), 1
    )
    for i in range(planes):
        own = jnp.broadcast_to(bc[i : i + 1, :].astype(F32), (columns, columns))
        column = jnp.sum(jnp.where(eye, own, 0.0), axis=1, keepdims=True)
        codes[i] = jnp.broadcast_to(column, (columns, LANE))


def pick(is_odd, pair, even_ref, idx):
    if len(pair) == 1:
        keep = is_odd if even_ref == 1 else jnp.logical_not(is_odd)
        return jnp.where(keep, pair[0][idx], 0.0)
    return jnp.where(is_odd, pair[1 - even_ref][idx], pair[even_ref][idx])


def make_plane(v, g, src, pre, jac, codes, put, spans, g_spans, span_at=None):
    span_odd = odd("span")

    def rows_of(even_ref, i):
        def get(c, kb):
            pair = g_spans if c == NV else spans
            k = i if c == NV or span_at is None else span_at
            one = pick(span_odd, pair, even_ref, (c, k, slice(None), pl.ds(kb * LANE, LANE)))
            return jnp.broadcast_to(one, (SUB, LANE))

        return get

    def plane(i, ssq, inside=None, halo=None, g_halo=None, sign=None, real=None):
        if halo is None:
            prev = lambda c, *sl: v[(c, i - 1, *sl)]
            nxt = lambda c, *sl: v[(c, i + 1, *sl)]
            gprev = lambda *sl: g[(i - 1, *sl)]
            gnxt = lambda *sl: g[(i + 1, *sl)]
        else:
            prev = lambda c, *sl: v[(c, inside, *sl)]
            nxt = lambda c, *sl: real * halo[(c, *sl)]
            gprev = lambda *sl: g[(inside, *sl)]
            gnxt = lambda *sl: real * g_halo[(NV, *sl)]
        return sweep_plane(
            i, v, prev, nxt, sign, g, gprev, gnxt, rows_of(1, i), rows_of(0, i), src, pre, jac,
            lambda jb: codes[i, pl.ds(jb * SUB, SUB), :],
            functools.partial(put, i),
            ssq,
        )

    return plane


def edge_of(pair, planes):
    low = odd("stream") if pair == 0 else jnp.logical_not(odd("stream"))
    return (
        jnp.where(low, 0, planes - 1),
        jnp.where(low, 1, planes - 2),
        jnp.where(low, -1.0, 1.0).astype(F32),
    )


def no_sum():
    return jnp.zeros((SUB, LANE), F32)


def first_inner(n_span, v, flow, src_hbm, pre_hbm, jac_in, bc, *refs):
    spans = refs[:n_span]
    out, g, src, pre, codes, jac, ssq_out = refs[n_span : n_span + 7]
    span_out, sem = refs[n_span + 7 : -1], refs[-1]
    planes = v.shape[1]

    def load(n, i):
        source, target = ((src_hbm, src), (pre_hbm, pre))[n]
        at = (slice(None),) * (n + 1) + (i,)
        return pltpu.make_async_copy(source.at[at], target.at[at], sem.at[n, i])

    order = [*range(1, planes - 1), 0, planes - 1]
    for i in order:
        load(0, i).start()
        load(1, i).start()
    spread_codes(bc, codes)
    for d in range(3):
        for u in range(NV):
            for c in range(NV):
                jac[(d * NV + u) * NV + c] = jnp.broadcast_to(
                    0.5 * jac_in[d, u : u + 1, c : c + 1], (SUB, LANE)
                )

    def speed_plane(i, carry):
        g[i] = quarter_speed(*[flow[c, i] for c in range(NV)])
        return carry

    lax.fori_loop(0, planes, speed_plane, 0)

    def put(i, c, sl, a):
        out[(c, i, *sl)] = a

    plane = make_plane(v, g, src, pre, jac, codes, put, spans, spans)

    def inner(i, ssq):
        load(0, i).wait()
        load(1, i).wait()
        ssq = plane(i, ssq)
        for c in range(NV):
            span_rows(out, c, i, span_out, i)
        return ssq

    ssq_out[...] = lax.fori_loop(1, planes - 1, inner, no_sum())
    for i in (0, planes - 1):
        load(0, i).wait()
        load(1, i).wait()


def first_edge(pair, n_span, v, g, src, pre, jac, codes, ssq_in, out_in, halo, *refs):
    spans = refs[:n_span]
    out, ssq_out, face = refs[n_span : n_span + 3]
    span_out = refs[n_span + 3 :]
    planes = v.shape[1]

    def put(i, c, sl, a):
        out[(c, i, *sl)] = a
        face[(c, *sl)] = a

    plane = make_plane(v, g, src, pre, jac, codes, put, spans, spans)
    i, inside, sign = edge_of(pair, planes)
    ssq_out[...] = plane(i, ssq_in[...], inside, halo, halo, sign, partner_at(pair))
    if pair == 1:
        for k in range(2):
            at = edge_of(k, planes)[0]
            for c in range(NV):
                span_rows(out, c, at, span_out, k)


def second_inner(n_span, v, g, src, pre, jac, codes, *refs):
    spans, g_spans = refs[:n_span], refs[n_span : 2 * n_span]
    out_hbm, ssq_out, out, sem = refs[2 * n_span :]
    planes = v.shape[1]

    def put(i, c, sl, a):
        out[(c, i, *sl)] = a

    plane = make_plane(v, g, src, pre, jac, codes, put, spans, g_spans)

    def store(i):
        return pltpu.make_async_copy(out.at[:, i], out_hbm.at[:, i], sem.at[i])

    def inner(i, ssq):
        ssq = plane(i, ssq)
        store(i).start()
        return ssq

    ssq_out[...] = lax.fori_loop(1, planes - 1, inner, no_sum())

    def finish(i, carry):
        store(i).wait()
        return carry

    lax.fori_loop(1, planes - 1, finish, 0)


def second_edge(pair, n_span, v, g, src, pre, jac, codes, ssq_in, halo, g_halo, *refs):
    spans, g_spans = refs[:n_span], refs[n_span : 2 * n_span]
    refs = refs[2 * n_span :]
    planes = v.shape[1]
    i, inside, sign = edge_of(pair, planes)
    ssq_before = refs[0] if pair == 1 else None
    out, ssq_out = refs[-2:]

    def put(i, c, sl, a):
        out[(c, *sl)] = a

    plane = make_plane(v, g, src, pre, jac, codes, put, spans, g_spans, pair)
    ssq = plane(i, ssq_in[...], inside, halo, g_halo, sign, partner_at(pair))
    if pair == 0:
        ssq_out[...] = ssq
        return
    lane = lax.broadcasted_iota(jnp.int32, ssq_out.shape, 1)
    before, now = jnp.sum(ssq_before[...]), jnp.sum(ssq)
    ssq_out[...] = jnp.where(lane == 0, before, jnp.where(lane == 1, now, 0.0))


def tail_kernel(cells_all, sums, edge_a, edge_b, result_in, result, rms, sem):
    ends = face_planes(result.shape[1])
    stores = [
        pltpu.make_async_copy(edge, result.at[:, end], sem.at[k])
        for k, (edge, end) in enumerate(zip((edge_a, edge_b), ends))
    ]
    for store in stores:
        store.start()
    total = jnp.sum(sums[...], axis=0, keepdims=True)
    rms[...] = jnp.sqrt(total / cells_all)[:, : rms.shape[1]]
    for store in stores:
        store.wait()


def pairs(count, offset):
    both = []
    for i in range(offset, count - 1, 2):
        both += [(i, i + 1), (i + 1, i)]
    return both


def exchange_pair(face, axis, pair):
    return lax.ppermute(face, axis, pairs(lax.axis_size(axis), pair))


def exchange_stream(face, pair):
    streams, spans = lax.axis_size("stream"), lax.axis_size("span")
    along = dict(pairs(streams, pair))
    across = dict(pairs(spans, 0))
    moves = []
    for i in range(streams):
        for j in range(spans):
            if i in along:
                moves.append((i * spans + j, along[i] * spans + j))
            elif j in across:
                moves.append((i * spans + j, i * spans + across[j]))
    return lax.ppermute(face, ("stream", "span"), moves)


def partner_at(pair):
    at, count = lax.axis_index("stream"), lax.axis_size("stream")
    is_odd = odd("stream")
    other = jnp.where(is_odd, at - 1, at + 1) if pair == 0 else jnp.where(is_odd, at + 1, at - 1)
    return jnp.where((other >= 0) & (other < count), 1.0, 0.0).astype(F32)


def exchange(faces, axis):
    return [exchange_pair(face, axis, pair) for pair, face in enumerate(faces)]


def per_device(adjoint_start, source, flow_state, precond, flux_jac, bc_codes):
    _, planes, rows, lanes = adjoint_start.shape
    n_stream, n_span_all = lax.axis_size("stream"), lax.axis_size("span")
    n_devices = n_stream * n_span_all
    n_span = 1 if n_span_all <= 2 else 2
    cells = planes * rows * lanes
    field = shape(NV, planes, rows, lanes)
    tile = shape(SUB, LANE)
    dma = pltpu.SemaphoreType.DMA
    inner_cost = cost(3000 * cells, 4 * cells, 42 * 4 * cells)
    edge_cost = cost(100 * cells, 0, 42 * cells)

    v, flow, *faces = pl.pallas_call(
        functools.partial(pack_kernel, n_span),
        out_shape=[field, field]
        + [shape(NV + 1, rows, lanes)] * 2
        + [shape(NV + 1, planes, 1, lanes)] * n_span,
        in_specs=[HBM] * 2,
        out_specs=[VMEM] * (4 + n_span),
        scratch_shapes=[pltpu.VMEM((NV, planes, 1, lanes), F32)] * n_span + [dma((2, 3))],
        cost_estimate=cost(cells, 0, 8 * cells),
        compiler_params=params(),
        name="pack",
    )(*hold(adjoint_start, flow_state, space=pltpu.HBM))
    streams = []
    for pair, face in enumerate(faces[:2]):
        streams.append(exchange_stream(face, pair))
    spans = exchange(faces[2:], "span")

    adjoint, g, src, pre, codes, jac, ssq, *rows_out = pl.pallas_call(
        functools.partial(first_inner, n_span),
        out_shape=[
            field, shape(planes, rows, lanes), field,
            shape(NV, NV, planes, rows, lanes), shape(planes, rows, LANE), shape(3 * NV * NV, SUB, LANE), tile,
        ]
        + [shape(NV, planes, 1, lanes)] * n_span,
        in_specs=[VMEM] * 2 + [HBM] * 2 + [VMEM] * (2 + n_span),
        out_specs=[VMEM] * (7 + n_span),
        scratch_shapes=[dma((2, planes))],
        cost_estimate=inner_cost,
        compiler_params=params(),
        name="first_inner",
    )(
        *hold(v, flow), *hold(source, precond, space=pltpu.HBM), *hold(flux_jac, bc_codes, *spans)
    )
    spans_inner = exchange(rows_out, "span")

    streams_next = []
    for pair in range(2):
        n_out = n_span if pair == 1 else 0
        first_edge_call = pl.pallas_call(
            functools.partial(first_edge, pair, n_span),
            out_shape=[field, tile, shape(NV, rows, lanes)] + [shape(NV, 2, 1, lanes)] * n_out,
            in_specs=[VMEM] * 5 + [VMEM] * (4 + n_span),
            out_specs=[VMEM] * (3 + n_out),
            input_output_aliases={7: 0},
            cost_estimate=edge_cost,
            compiler_params=params(),
        )
        adjoint, ssq, face, *rows_out = first_edge_call(
            *hold(v, g, src, pre, jac, codes, ssq, adjoint, streams[pair], *spans)
        )
        streams_next.append(exchange_stream(face, pair))
    ssq_first = ssq
    spans_edge = exchange(rows_out, "span")

    result, ssq = pl.pallas_call(
        functools.partial(second_inner, n_span),
        out_shape=[pltpu.HBM(adjoint_start.shape, F32), tile],
        in_specs=[VMEM] * 5 + [VMEM] * (1 + 2 * n_span),
        out_specs=[HBM, VMEM],
        scratch_shapes=[field, dma((planes,))],
        cost_estimate=inner_cost,
        compiler_params=params(),
        name="second_inner",
    )(*hold(adjoint, g, src, pre, jac), *hold(codes, *spans_inner, *spans))

    face = shape(NV, rows, lanes)
    edges = []
    for pair in range(2):
        edge, ssq = pl.pallas_call(
            functools.partial(second_edge, pair, n_span),
            out_shape=[face, shape(n_devices, LANE) if pair else tile],
            in_specs=[VMEM] * (9 + 2 * n_span + pair),
            out_specs=[VMEM] * 2,
            cost_estimate=edge_cost,
            compiler_params=params(),
        )(
            *hold(adjoint, g, src, pre, jac, codes, ssq, streams_next[pair], streams[pair]),
            *hold(*spans_edge, *spans, *([ssq_first] * pair)),
        )
        edges.append(edge)
    sums = lax.all_to_all(ssq, ("stream", "span"), 0, 0, tiled=True)
    result, rms = pl.pallas_call(
        functools.partial(tail_kernel, float(NV * cells * n_devices)),
        out_shape=[pltpu.HBM(adjoint_start.shape, F32), jax.ShapeDtypeStruct((1, 2), F32)],
        in_specs=[VMEM] * 3 + [HBM],
        out_specs=[HBM, VMEM],
        scratch_shapes=[dma((2,))],
        input_output_aliases={3: 0},
        compiler_params=params(),
        name="tail",
    )(*hold(sums, *edges), *hold(result, space=pltpu.HBM))
    return (result, rms.reshape(2))


def solution(mesh):
    in_specs = (
        P(None, "stream", "span", None),
        P(None, "stream", "span", None),
        P(None, "stream", "span", None),
        P(None, None, "stream", "span", None),
        P(),
        P("stream", "span"),
    )
    out_specs = (P(None, "stream", "span", None), P())

    return jax.shard_map(
        per_device, mesh=mesh, in_specs=in_specs, out_specs=out_specs, check_vma=False
    )
```

```python
import functools

import jax
import jax.numpy as jnp
from jax import lax
from jax.experimental import pallas as pl
from jax.experimental.pallas import tpu as pltpu
from jax.sharding import PartitionSpec as P


NV = 5
SWEEPS = 2
SUB, LANE = 8, 128
F32 = jnp.float32
ORDER = (1, 0)
VMEM = pl.BlockSpec(memory_space=pltpu.VMEM)
HBM = pl.BlockSpec(memory_space=pltpu.HBM)


def shape(*dims):
    return pltpu.VMEM(dims, F32)


def hold(*arrays, space=pltpu.VMEM):
    return [pltpu.with_memory_space_constraint(a, space) for a in arrays]


def params():
    return pltpu.CompilerParams(vmem_limit_bytes=4 << 20)


def cost(flops, transcendentals, bytes_accessed):
    return pl.CostEstimate(
        flops=int(flops), transcendentals=int(transcendentals), bytes_accessed=int(bytes_accessed)
    )


def quarter_speed(rho, m1, m2, m3, p):
    momentum = jnp.sqrt(m1 * m1 + m2 * m2 + m3 * m3)
    return 0.25 * (momentum / rho + jnp.sqrt(1.4 * p / rho))


def odd(axis):
    return lax.rem(lax.axis_index(axis), 2) == 1


def face_planes(planes):
    is_odd = odd("stream")
    return jnp.where(is_odd, 0, planes - 1), jnp.where(is_odd, planes - 1, 0)


def span_rows(field, c, i, out_refs, k):
    is_odd = odd("span")
    last = field.shape[-2] - 1
    at = (i,) if c is None else (c, i)
    to = (k,) if c is None else (c, k)
    head = field[(*at, slice(0, 1))]
    tail = field[(*at, slice(last, last + 1))]
    out_refs[0][to] = jnp.where(is_odd, head, tail)
    if len(out_refs) > 1:
        out_refs[1][to] = jnp.where(is_odd, tail, head)


def pack_kernel(v_hbm, flow_hbm, fa, fb, face_in, sem):
    ends = face_planes(v_hbm.shape[1])
    faces = (fa, fb)
    fields = (flow_hbm, v_hbm)
    loads = [
        [
            pltpu.make_async_copy(field.at[:, ends[pair]], face_in.at[pair, n], sem.at[pair, n])
            for n, field in enumerate(fields)
        ]
        for pair in range(2)
    ]
    for pair in ORDER:
        for load in loads[pair]:
            load.start()
    for pair in ORDER:
        for load in loads[pair]:
            load.wait()
        faces[pair][NV] = quarter_speed(*[face_in[pair, 0, c] for c in range(NV)])
        for c in range(NV):
            faces[pair][c] = face_in[pair, 1, c]


def plane_loads(src_hbm, pre_hbm, src, pre, sem, i):
    return (
        pltpu.make_async_copy(src_hbm.at[:, i], src.at[:, i], sem.at[0, i]),
        pltpu.make_async_copy(pre_hbm.at[:, :, i], pre.at[:, :, i], sem.at[1, i]),
    )


def load_kernel(n_span, v_hbm, flow_hbm, src_hbm, pre_hbm, jac_in, bc, *refs):
    v, g, src, pre, codes, jac = refs[:6]
    spans, (flow, sem) = refs[6 : 6 + n_span], refs[6 + n_span :]
    planes = v.shape[1]
    loads = [
        [
            pltpu.make_async_copy(source.at[:, i], target.at[:, i], sem.at[n, i])
            for n, (source, target) in enumerate(((flow_hbm, flow), (v_hbm, v)))
        ]
        for i in range(planes)
    ]
    early = plane_loads(src_hbm, pre_hbm, src, pre, sem.at[pl.ds(2, 2)], 1)
    for load in [load for pair in loads for load in pair] + [*early]:
        load.start()
    spread_codes(bc, codes)
    for d in range(3):
        for u in range(NV):
            for c in range(NV):
                jac[(d * NV + u) * NV + c] = jnp.broadcast_to(
                    0.5 * jac_in[d, u : u + 1, c : c + 1], (SUB, LANE)
                )
    for i in range(planes):
        for load in loads[i]:
            load.wait()
        g[i] = quarter_speed(*[flow[c, i] for c in range(NV)])
        for c in range(NV):
            span_rows(v, c, i, spans, i)
    for i in range(planes):
        span_rows(g, None, i, [span.at[NV] for span in spans], i)
    for load in early:
        load.wait()


def sweep_plane(i, v, prev, nxt, sign, g, gprev, gnxt, tops, bottoms, src, pre, jac, wall, put, ssq):
    rows_n, lanes_n = v.shape[2] // SUB, v.shape[3] // LANE
    lane = lax.broadcasted_iota(jnp.int32, (SUB, LANE), 1)
    row = lax.broadcasted_iota(jnp.int32, (SUB, LANE), 0)
    first_lane, last_lane = lane == 0, lane == LANE - 1
    first_row, last_row = row == 0, row == SUB - 1
    zero = jnp.zeros((SUB, LANE), F32)

    def at(jb, kb):
        return pl.ds(jb * SUB, SUB), pl.ds(kb * LANE, LANE)

    def shifts(get):
        @functools.cache
        def turned(jb, kb, shift, axis):
            return pltpu.roll(tile(jb, kb), shift % (SUB, LANE)[axis], axis)

        @functools.cache
        def tile(jb, kb):
            return get(*at(jb, kb))

        def shifted(top, bottom, jb, kb):
            before = top(kb) if jb == 0 else turned(jb - 1, kb, 1, 0)
            after = bottom(kb) if jb == rows_n - 1 else turned(jb + 1, kb, -1, 0)
            low = zero if kb == 0 else turned(jb, kb - 1, 1, 1)
            high = zero if kb == lanes_n - 1 else turned(jb, kb + 1, -1, 1)
            return (
                tile(jb, kb),
                jnp.where(first_row, before, turned(jb, kb, 1, 0)),
                jnp.where(last_row, after, turned(jb, kb, -1, 0)),
                jnp.where(first_lane, low, turned(jb, kb, 1, 1)),
                jnp.where(last_lane, high, turned(jb, kb, -1, 1)),
            )

        return shifted

    g_shift = shifts(lambda *sl: g[(i, *sl)])
    v_shift = [shifts(lambda *sl, c=c: v[(c, i, *sl)]) for c in range(NV)]
    total = ssq
    for kb in range(lanes_n):
        for jb in range(rows_n):
            sl = at(jb, kb)
            gs, gu, gd, gl, gr = g_shift(
                functools.partial(tops, NV), functools.partial(bottoms, NV), jb, kb
            )
            coefs = [gs + gprev(*sl), gs + gnxt(*sl), gs + gu, gs + gd, gs + gl, gs + gr]
            diag = ((coefs[0] + coefs[1]) + (coefs[2] + coefs[3])) + (coefs[4] + coefs[5])
            diffs, owns, res = [], [], []
            for c in range(NV):
                own, up, down, left, right = v_shift[c](
                    functools.partial(tops, c), functools.partial(bottoms, c), jb, kb
                )
                before, after = prev(c, *sl), nxt(c, *sl)
                across = before - after if sign is None else sign * (before - after)
                diffs.append((across, up - down, left - right))
                owns.append(own)
                pulls = (
                    (coefs[0] * before + coefs[1] * after)
                    + (coefs[2] * up + coefs[3] * down)
                ) + (coefs[4] * left + coefs[5] * right)
                res.append(src[(c, i, *sl)] - (diag * own - pulls))
            for c in range(NV):
                r = res[c]
                for d in range(3):
                    for u in range(NV):
                        r = r - jac[(d * NV + u) * NV + c] * diffs[u][d]
                res[c] = r
            if kb == 0:
                code = wall(jb)
                on_wall = first_lane & (code != 1)
                for c in range(NV):
                    t = gs * owns[c]
                    for u in range(NV):
                        t = t + jac[(2 * NV + u) * NV + c] * owns[u]
                    if c == 3:
                        t = jnp.where(code == 0, -t, t)
                    res[c] = res[c] + jnp.where(on_wall, t, zero)
            for c in range(NV):
                total = total + res[c] * res[c]
            for c in range(NV):
                a = owns[c]
                for u in range(NV):
                    a = a + pre[(u, c, i, *sl)] * res[u]
                put(c, sl, a)
    return total


def spread_codes(bc, codes):
    planes, columns = bc.shape
    eye = lax.broadcasted_iota(jnp.int32, (columns, columns), 0) == lax.broadcasted_iota(
        jnp.int32, (columns, columns), 1
    )
    for i in range(planes):
        own = jnp.broadcast_to(bc[i : i + 1, :].astype(F32), (columns, columns))
        column = jnp.sum(jnp.where(eye, own, 0.0), axis=1, keepdims=True)
        codes[i] = jnp.broadcast_to(column, (columns, LANE))


def pick(is_odd, pair, even_ref, idx):
    if len(pair) == 1:
        keep = is_odd if even_ref == 1 else jnp.logical_not(is_odd)
        return jnp.where(keep, pair[0][idx], 0.0)
    return jnp.where(is_odd, pair[1 - even_ref][idx], pair[even_ref][idx])


def make_plane(v, g, src, pre, jac, codes, put, spans, g_spans, span_at=None):
    span_odd = odd("span")

    def rows_of(even_ref, i):
        def get(c, kb):
            pair = g_spans if c == NV else spans
            k = i if c == NV or span_at is None else span_at
            one = pick(span_odd, pair, even_ref, (c, k, slice(None), pl.ds(kb * LANE, LANE)))
            return jnp.broadcast_to(one, (SUB, LANE))

        return get

    def plane(i, ssq, inside=None, halo=None, g_halo=None, sign=None, real=None):
        if halo is None:
            prev = lambda c, *sl: v[(c, i - 1, *sl)]
            nxt = lambda c, *sl: v[(c, i + 1, *sl)]
            gprev = lambda *sl: g[(i - 1, *sl)]
            gnxt = lambda *sl: g[(i + 1, *sl)]
        else:
            prev = lambda c, *sl: v[(c, inside, *sl)]
            nxt = lambda c, *sl: real * halo[(c, *sl)]
            gprev = lambda *sl: g[(inside, *sl)]
            gnxt = lambda *sl: real * g_halo[(NV, *sl)]
        return sweep_plane(
            i, v, prev, nxt, sign, g, gprev, gnxt, rows_of(1, i), rows_of(0, i), src, pre, jac,
            lambda jb: codes[i, pl.ds(jb * SUB, SUB), :],
            functools.partial(put, i),
            ssq,
        )

    return plane


def edge_of(pair, planes):
    low = odd("stream") if pair == 0 else jnp.logical_not(odd("stream"))
    return (
        jnp.where(low, 0, planes - 1),
        jnp.where(low, 1, planes - 2),
        jnp.where(low, -1.0, 1.0).astype(F32),
    )


def no_sum():
    return jnp.zeros((SUB, LANE), F32)


def first_inner(n_span, part, v, g, jac, codes, src_hbm, pre_hbm, src_in, pre_in, *refs):
    spans = refs[:n_span]
    out, src, pre, ssq_out, sem = refs[n_span:]
    planes = v.shape[1]

    def loads(i):
        return plane_loads(src_hbm, pre_hbm, src, pre, sem, i)

    late = [*range(2, planes - 1), 0, planes - 1]
    for i in late:
        for load in loads(i):
            load.start()

    def put(i, c, sl, a):
        out[(c, i, *sl)] = a

    plane = make_plane(v, g, src, pre, jac, codes, put, spans, spans)

    def inner(i, ssq):
        @pl.when(i > 1)
        def _():
            for load in loads(i):
                load.wait()

        return plane(i, ssq)

    ssq_out[...] = lax.fori_loop(1, part, inner, no_sum())
    for i in late[part - 2 :]:
        for load in loads(i):
            load.wait()


def first_rest(n_span, part, v, g, src, pre, jac, codes, ssq_in, out_in, *refs):
    spans = refs[:n_span]
    out, ssq_out = refs[n_span : n_span + 2]
    span_out = refs[n_span + 2 :]
    planes = v.shape[1]

    def put(i, c, sl, a):
        out[(c, i, *sl)] = a

    plane = make_plane(v, g, src, pre, jac, codes, put, spans, spans)
    ssq_out[...] = lax.fori_loop(part, planes - 1, plane, ssq_in[...])
    for i in range(1, planes - 1):
        for c in range(NV):
            span_rows(out, c, i, span_out, i)


def first_edge(pair, n_span, v, g, src, pre, jac, codes, ssq_in, out_in, halo, *refs):
    spans = refs[:n_span]
    out, ssq_out, face = refs[n_span : n_span + 3]
    span_out = refs[n_span + 3 :]
    planes = v.shape[1]

    def put(i, c, sl, a):
        out[(c, i, *sl)] = a
        face[(c, *sl)] = a

    plane = make_plane(v, g, src, pre, jac, codes, put, spans, spans)
    i, inside, sign = edge_of(pair, planes)
    ssq_out[...] = plane(i, ssq_in[...], inside, halo, halo, sign, partner_at(pair))
    if pair == ORDER[1]:
        for k in range(2):
            at = edge_of(k, planes)[0]
            for c in range(NV):
                span_rows(out, c, at, span_out, k)


def second_inner(n_span, v, g, src, pre, jac, codes, *refs):
    spans, g_spans = refs[:n_span], refs[n_span : 2 * n_span]
    out_hbm, ssq_out, out, sem = refs[2 * n_span :]
    planes = v.shape[1]

    def put(i, c, sl, a):
        out[(c, i, *sl)] = a

    plane = make_plane(v, g, src, pre, jac, codes, put, spans, g_spans)

    def store(i):
        return pltpu.make_async_copy(out.at[:, i], out_hbm.at[:, i], sem.at[i])

    def inner(i, ssq):
        ssq = plane(i, ssq)
        store(i).start()
        return ssq

    ssq_out[...] = lax.fori_loop(1, planes - 1, inner, no_sum())

    def finish(i, carry):
        store(i).wait()
        return carry

    lax.fori_loop(1, planes - 1, finish, 0)


def second_edge(pair, n_span, v, g, src, pre, jac, codes, ssq_in, halo, g_halo, *refs):
    spans, g_spans = refs[:n_span], refs[n_span : 2 * n_span]
    refs = refs[2 * n_span :]
    planes = v.shape[1]
    i, inside, sign = edge_of(pair, planes)
    last = pair == ORDER[1]
    out, ssq_out = refs[-2:]

    def put(i, c, sl, a):
        out[(c, *sl)] = a

    plane = make_plane(v, g, src, pre, jac, codes, put, spans, g_spans, pair)
    ssq = plane(i, ssq_in[...], inside, halo, g_halo, sign, partner_at(pair))
    if not last:
        ssq_out[...] = ssq
        return
    lane = lax.broadcasted_iota(jnp.int32, ssq_out.shape, 1)
    before, now = jnp.sum(refs[0][...]), jnp.sum(ssq)
    ssq_out[...] = jnp.where(lane == 0, before, jnp.where(lane == 1, now, 0.0))


def tail_kernel(cells_all, sums, edge_a, edge_b, result_in, result, rms_hbm, rms, sem):
    ends = face_planes(result.shape[1])
    stores = [
        pltpu.make_async_copy(edge, result.at[:, end], sem.at[k])
        for k, (edge, end) in enumerate(zip((edge_a, edge_b), ends))
    ]
    total = jnp.sum(sums[...], axis=0, keepdims=True)
    for store in stores:
        store.start()
    rms[...] = jnp.sqrt(total / cells_all)[:, : rms.shape[1]]
    stores.append(pltpu.make_async_copy(rms, rms_hbm, sem.at[2]))
    stores[-1].start()
    for store in stores:
        store.wait()


def pairs(count, offset):
    both = []
    for i in range(offset, count - 1, 2):
        both += [(i, i + 1), (i + 1, i)]
    return both


def exchange_pair(face, axis, pair):
    return lax.ppermute(face, axis, pairs(lax.axis_size(axis), pair))


def exchange_stream(face, pair):
    streams, spans = lax.axis_size("stream"), lax.axis_size("span")
    along = dict(pairs(streams, pair))
    across = dict(pairs(spans, 0))
    moves = []
    for i in range(streams):
        for j in range(spans):
            if i in along:
                moves.append((i * spans + j, along[i] * spans + j))
            elif j in across:
                moves.append((i * spans + j, i * spans + across[j]))
    return lax.ppermute(face, ("stream", "span"), moves)


def partner_at(pair):
    at, count = lax.axis_index("stream"), lax.axis_size("stream")
    is_odd = odd("stream")
    other = jnp.where(is_odd, at - 1, at + 1) if pair == 0 else jnp.where(is_odd, at + 1, at - 1)
    return jnp.where((other >= 0) & (other < count), 1.0, 0.0).astype(F32)


def exchange(faces, axis):
    return [exchange_pair(face, axis, pair) for pair, face in enumerate(faces)]


def per_device(adjoint_start, source, flow_state, precond, flux_jac, bc_codes):
    _, planes, rows, lanes = adjoint_start.shape
    n_stream, n_span_all = lax.axis_size("stream"), lax.axis_size("span")
    n_devices = n_stream * n_span_all
    n_span = 1 if n_span_all <= 2 else 2
    cells = planes * rows * lanes
    field = shape(NV, planes, rows, lanes)
    tile = shape(SUB, LANE)
    dma = pltpu.SemaphoreType.DMA
    inner_cost = cost(3000 * cells, 4 * cells, 42 * 4 * cells)
    edge_cost = cost(100 * cells, 0, 42 * cells)

    faces = pl.pallas_call(
        pack_kernel,
        out_shape=[shape(NV + 1, rows, lanes)] * 2,
        in_specs=[HBM] * 2,
        out_specs=[VMEM] * 2,
        scratch_shapes=[shape(2, 2, NV, rows, lanes), dma((2, 2))],
        cost_estimate=cost(cells, 0, 8 * cells),
        compiler_params=params(),
        name="pack",
    )(*hold(adjoint_start, flow_state, space=pltpu.HBM))
    streams = []
    for pair, face in enumerate(faces):
        streams.append(exchange_stream(face, pair))

    load_call = pl.pallas_call(
        functools.partial(load_kernel, n_span),
        out_shape=[
            field, shape(planes, rows, lanes), field, shape(NV, NV, planes, rows, lanes),
            shape(planes, rows, LANE), shape(3 * NV * NV, SUB, LANE),
        ]
        + [shape(NV + 1, planes, 1, lanes)] * n_span,
        in_specs=[HBM] * 4 + [VMEM] * 2,
        out_specs=[VMEM] * (6 + n_span),
        scratch_shapes=[field, dma((4, planes))],
        cost_estimate=inner_cost,
        compiler_params=params(),
        name="load",
    )
    v, g, src, pre, codes, jac, *rows_out = load_call(
        *hold(adjoint_start, flow_state, source, precond, space=pltpu.HBM),
        *hold(flux_jac, bc_codes),
    )
    spans = exchange(rows_out, "span")

    part = 1 + max((planes - 2) * 2 // 3, 1)
    first_call = pl.pallas_call(
        functools.partial(first_inner, n_span, part),
        out_shape=[field, field, shape(NV, NV, planes, rows, lanes), tile],
        in_specs=[VMEM] * 4 + [HBM] * 2 + [VMEM] * (2 + n_span),
        out_specs=[VMEM] * 4,
        scratch_shapes=[dma((2, planes))],
        input_output_aliases={6: 1, 7: 2},
        cost_estimate=inner_cost,
        compiler_params=params(),
        name="first_inner",
    )
    adjoint, src, pre, ssq = first_call(
        *hold(v, g, jac, codes), *hold(source, precond, space=pltpu.HBM), *hold(src, pre, *spans)
    )

    def first_edge_call(pair, adjoint, ssq):
        n_out = n_span if pair == ORDER[1] else 0
        edge_call = pl.pallas_call(
            functools.partial(first_edge, pair, n_span),
            out_shape=[field, tile, shape(NV, rows, lanes)] + [shape(NV, 2, 1, lanes)] * n_out,
            in_specs=[VMEM] * (9 + n_span),
            out_specs=[VMEM] * (3 + n_out),
            input_output_aliases={7: 0},
            cost_estimate=edge_cost,
            compiler_params=params(),
        )
        adjoint, ssq, face, *rows_out = edge_call(
            *hold(v, g, src, pre, jac, codes, ssq, adjoint, streams[pair], *spans)
        )
        return adjoint, ssq, exchange_stream(face, pair), rows_out

    streams_next = [None, None]
    adjoint, ssq, streams_next[ORDER[0]], _ = first_edge_call(ORDER[0], adjoint, ssq)
    rest_call = pl.pallas_call(
        functools.partial(first_rest, n_span, part),
        out_shape=[field, tile] + [shape(NV, planes, 1, lanes)] * n_span,
        in_specs=[VMEM] * (8 + n_span),
        out_specs=[VMEM] * (2 + n_span),
        input_output_aliases={7: 0},
        cost_estimate=inner_cost,
        compiler_params=params(),
        name="first_rest",
    )
    adjoint, ssq, *rows_out = rest_call(*hold(v, g, src, pre, jac, codes, ssq, adjoint, *spans))
    spans_inner = exchange(rows_out, "span")
    adjoint, ssq, streams_next[ORDER[1]], rows_out = first_edge_call(ORDER[1], adjoint, ssq)
    ssq_first = ssq
    spans_edge = exchange(rows_out, "span")

    second_call = pl.pallas_call(
        functools.partial(second_inner, n_span),
        out_shape=[pltpu.HBM(adjoint_start.shape, F32), tile],
        in_specs=[VMEM] * (6 + 2 * n_span),
        out_specs=[HBM, VMEM],
        scratch_shapes=[field, dma((planes,))],
        cost_estimate=inner_cost,
        compiler_params=params(),
        name="second_inner",
    )
    result, ssq = second_call(*hold(adjoint, g, src, pre, jac, codes, *spans_inner, *spans))

    face = shape(NV, rows, lanes)
    edges = [None, None]
    for pair in ORDER:
        last = pair == ORDER[1]
        edge_call = pl.pallas_call(
            functools.partial(second_edge, pair, n_span),
            out_shape=[face, shape(n_devices, LANE) if last else tile],
            in_specs=[VMEM] * (9 + 2 * n_span + last),
            out_specs=[VMEM] * 2,
            cost_estimate=edge_cost,
            compiler_params=params(),
        )
        edges[pair], ssq = edge_call(
            *hold(adjoint, g, src, pre, jac, codes, ssq, streams_next[pair], streams[pair]),
            *hold(*spans_edge, *spans, *([ssq_first] * last)),
        )
    sums = lax.all_to_all(ssq, ("stream", "span"), 0, 0, tiled=True)
    result, rms = pl.pallas_call(
        functools.partial(tail_kernel, float(NV * cells * n_devices)),
        out_shape=[pltpu.HBM(adjoint_start.shape, F32), pltpu.HBM((1, SWEEPS), F32)],
        in_specs=[VMEM] * 3 + [HBM],
        out_specs=[HBM] * 2,
        scratch_shapes=[shape(1, SWEEPS), dma((3,))],
        input_output_aliases={3: 0},
        compiler_params=params(),
        name="tail",
    )(*hold(sums, *edges), *hold(result, space=pltpu.HBM))
    return (result, rms.reshape(SWEEPS))


def solution(mesh):
    in_specs = (
        P(None, "stream", "span", None),
        P(None, "stream", "span", None),
        P(None, "stream", "span", None),
        P(None, None, "stream", "span", None),
        P(),
        P("stream", "span"),
    )
    out_specs = (P(None, "stream", "span", None), P())

    return jax.shard_map(
        per_device, mesh=mesh, in_specs=in_specs, out_specs=out_specs, check_vma=False
    )
```

```python
import functools

import jax
import jax.numpy as jnp
from jax import lax
from jax.experimental import pallas as pl
from jax.experimental.pallas import tpu as pltpu
from jax.sharding import PartitionSpec as P


NV = 5
SWEEPS = 2
SUB, LANE = 8, 128
F32 = jnp.float32
ORDER = (1, 0)
VMEM = pl.BlockSpec(memory_space=pltpu.VMEM)
HBM = pl.BlockSpec(memory_space=pltpu.HBM)


def shape(*dims):
    return pltpu.VMEM(dims, F32)


def hold(*arrays, space=pltpu.VMEM):
    return [pltpu.with_memory_space_constraint(a, space) for a in arrays]


def params():
    return pltpu.CompilerParams(vmem_limit_bytes=4 << 20)


def cost(flops, transcendentals, bytes_accessed):
    return pl.CostEstimate(
        flops=int(flops), transcendentals=int(transcendentals), bytes_accessed=int(bytes_accessed)
    )


def quarter_speed(rho, m1, m2, m3, p):
    momentum = jnp.sqrt(m1 * m1 + m2 * m2 + m3 * m3)
    return 0.25 * (momentum / rho + jnp.sqrt(1.4 * p / rho))


def odd(axis):
    return lax.rem(lax.axis_index(axis), 2) == 1


def face_planes(planes):
    is_odd = odd("stream")
    return jnp.where(is_odd, 0, planes - 1), jnp.where(is_odd, planes - 1, 0)


def span_rows(field, c, i, out_refs, k):
    is_odd = odd("span")
    last = field.shape[-2] - 1
    at = (i,) if c is None else (c, i)
    to = (k,) if c is None else (c, k)
    head = field[(*at, slice(0, 1))]
    tail = field[(*at, slice(last, last + 1))]
    out_refs[0][to] = jnp.where(is_odd, head, tail)
    if len(out_refs) > 1:
        out_refs[1][to] = jnp.where(is_odd, tail, head)


def fill_face(face, v, flow):
    face[NV] = quarter_speed(*[flow(c) for c in range(NV)])
    for c in range(NV):
        face[c] = v(c)


def pack_kernel(v_hbm, flow_hbm, face, flow_in, v_in, sem):
    end = face_planes(v_hbm.shape[1])[ORDER[0]]
    loads = [
        pltpu.make_async_copy(field.at[:, end], target, sem.at[n])
        for n, (field, target) in enumerate(((flow_hbm, flow_in), (v_hbm, v_in)))
    ]
    for load in loads:
        load.start()
    for load in loads:
        load.wait()
    fill_face(face, lambda c: v_in[c], lambda c: flow_in[c])


def plane_loads(src_hbm, pre_hbm, src, pre, sem, i):
    return (
        pltpu.make_async_copy(src_hbm.at[:, i], src.at[:, i], sem.at[0, i]),
        pltpu.make_async_copy(pre_hbm.at[:, :, i], pre.at[:, :, i], sem.at[1, i]),
    )


def load_kernel(n_span, v, flow, src_hbm, pre_hbm, jac_hbm, bc_hbm, *refs):
    g, src, pre, codes, jac, face = refs[:6]
    spans, (jac_in, bc, small, sem) = refs[6 : 6 + n_span], refs[6 + n_span :]
    planes = v.shape[1]
    tables = [
        pltpu.make_async_copy(jac_hbm, jac_in, small.at[0]),
        pltpu.make_async_copy(bc_hbm, bc, small.at[1]),
    ]
    early = plane_loads(src_hbm, pre_hbm, src, pre, sem, 1)
    for load in [*tables, *early]:
        load.start()
    end = face_planes(planes)[ORDER[1]]
    fill_face(face, lambda c: v[c, end], lambda c: flow[c, end])
    for i in range(planes):
        g[i] = quarter_speed(*[flow[c, i] for c in range(NV)])
        for c in range(NV):
            span_rows(v, c, i, spans, i)
    for i in range(planes):
        span_rows(g, None, i, [span.at[NV] for span in spans], i)
    for load in tables:
        load.wait()
    spread_codes(bc, codes)
    for d in range(3):
        for u in range(NV):
            for c in range(NV):
                jac[(d * NV + u) * NV + c] = jnp.broadcast_to(
                    0.5 * jac_in[u, d : d + 1, c : c + 1], (SUB, LANE)
                )
    for load in early:
        load.wait()


def sweep_plane(i, v, prev, nxt, sign, g, gprev, gnxt, tops, bottoms, src, pre, jac, wall, put, ssq):
    rows_n, lanes_n = v.shape[2] // SUB, v.shape[3] // LANE
    lane = lax.broadcasted_iota(jnp.int32, (SUB, LANE), 1)
    row = lax.broadcasted_iota(jnp.int32, (SUB, LANE), 0)
    first_lane, last_lane = lane == 0, lane == LANE - 1
    first_row, last_row = row == 0, row == SUB - 1
    zero = jnp.zeros((SUB, LANE), F32)

    def at(jb, kb):
        return pl.ds(jb * SUB, SUB), pl.ds(kb * LANE, LANE)

    def shifts(get):
        @functools.cache
        def turned(jb, kb, shift, axis):
            return pltpu.roll(tile(jb, kb), shift % (SUB, LANE)[axis], axis)

        @functools.cache
        def tile(jb, kb):
            return get(*at(jb, kb))

        def shifted(top, bottom, jb, kb):
            before = top(kb) if jb == 0 else turned(jb - 1, kb, 1, 0)
            after = bottom(kb) if jb == rows_n - 1 else turned(jb + 1, kb, -1, 0)
            low = zero if kb == 0 else turned(jb, kb - 1, 1, 1)
            high = zero if kb == lanes_n - 1 else turned(jb, kb + 1, -1, 1)
            return (
                tile(jb, kb),
                jnp.where(first_row, before, turned(jb, kb, 1, 0)),
                jnp.where(last_row, after, turned(jb, kb, -1, 0)),
                jnp.where(first_lane, low, turned(jb, kb, 1, 1)),
                jnp.where(last_lane, high, turned(jb, kb, -1, 1)),
            )

        return shifted

    g_shift = shifts(lambda *sl: g[(i, *sl)])
    v_shift = [shifts(lambda *sl, c=c: v[(c, i, *sl)]) for c in range(NV)]
    total = ssq
    for kb in range(lanes_n):
        for jb in range(rows_n):
            sl = at(jb, kb)
            gs, gu, gd, gl, gr = g_shift(
                functools.partial(tops, NV), functools.partial(bottoms, NV), jb, kb
            )
            coefs = [gs + gprev(*sl), gs + gnxt(*sl), gs + gu, gs + gd, gs + gl, gs + gr]
            diag = ((coefs[0] + coefs[1]) + (coefs[2] + coefs[3])) + (coefs[4] + coefs[5])
            diffs, owns, res = [], [], []
            for c in range(NV):
                own, up, down, left, right = v_shift[c](
                    functools.partial(tops, c), functools.partial(bottoms, c), jb, kb
                )
                before, after = prev(c, *sl), nxt(c, *sl)
                across = before - after if sign is None else sign * (before - after)
                diffs.append((across, up - down, left - right))
                owns.append(own)
                pulls = (
                    (coefs[0] * before + coefs[1] * after)
                    + (coefs[2] * up + coefs[3] * down)
                ) + (coefs[4] * left + coefs[5] * right)
                res.append(src[(c, i, *sl)] - (diag * own - pulls))
            for c in range(NV):
                r = res[c]
                for d in range(3):
                    for u in range(NV):
                        r = r - jac[(d * NV + u) * NV + c] * diffs[u][d]
                res[c] = r
            if kb == 0:
                code = wall(jb)
                on_wall = first_lane & (code != 1)
                for c in range(NV):
                    t = gs * owns[c]
                    for u in range(NV):
                        t = t + jac[(2 * NV + u) * NV + c] * owns[u]
                    if c == 3:
                        t = jnp.where(code == 0, -t, t)
                    res[c] = res[c] + jnp.where(on_wall, t, zero)
            for c in range(NV):
                total = total + res[c] * res[c]
            for c in range(NV):
                a = owns[c]
                for u in range(NV):
                    a = a + pre[(u, c, i, *sl)] * res[u]
                put(c, sl, a)
    return total


def spread_codes(bc, codes):
    planes, columns = bc.shape
    eye = lax.broadcasted_iota(jnp.int32, (columns, columns), 0) == lax.broadcasted_iota(
        jnp.int32, (columns, columns), 1
    )
    for i in range(planes):
        own = jnp.broadcast_to(bc[i : i + 1, :].astype(F32), (columns, columns))
        column = jnp.sum(jnp.where(eye, own, 0.0), axis=1, keepdims=True)
        codes[i] = jnp.broadcast_to(column, (columns, LANE))


def pick(is_odd, pair, even_ref, idx):
    if len(pair) == 1:
        keep = is_odd if even_ref == 1 else jnp.logical_not(is_odd)
        return jnp.where(keep, pair[0][idx], 0.0)
    return jnp.where(is_odd, pair[1 - even_ref][idx], pair[even_ref][idx])


def make_plane(v, g, src, pre, jac, codes, put, spans, g_spans, span_at=None):
    span_odd = odd("span")

    def rows_of(even_ref, i):
        def get(c, kb):
            pair = g_spans if c == NV else spans
            k = i if c == NV or span_at is None else span_at
            one = pick(span_odd, pair, even_ref, (c, k, slice(None), pl.ds(kb * LANE, LANE)))
            return jnp.broadcast_to(one, (SUB, LANE))

        return get

    def plane(i, ssq, inside=None, halo=None, g_halo=None, sign=None, real=None):
        if halo is None:
            prev = lambda c, *sl: v[(c, i - 1, *sl)]
            nxt = lambda c, *sl: v[(c, i + 1, *sl)]
            gprev = lambda *sl: g[(i - 1, *sl)]
            gnxt = lambda *sl: g[(i + 1, *sl)]
        else:
            prev = lambda c, *sl: v[(c, inside, *sl)]
            nxt = lambda c, *sl: real * halo[(c, *sl)]
            gprev = lambda *sl: g[(inside, *sl)]
            gnxt = lambda *sl: real * g_halo[(NV, *sl)]
        return sweep_plane(
            i, v, prev, nxt, sign, g, gprev, gnxt, rows_of(1, i), rows_of(0, i), src, pre, jac,
            lambda jb: codes[i, pl.ds(jb * SUB, SUB), :],
            functools.partial(put, i),
            ssq,
        )

    return plane


def edge_of(pair, planes):
    low = odd("stream") if pair == 0 else jnp.logical_not(odd("stream"))
    return (
        jnp.where(low, 0, planes - 1),
        jnp.where(low, 1, planes - 2),
        jnp.where(low, -1.0, 1.0).astype(F32),
    )


def no_sum():
    return jnp.zeros((SUB, LANE), F32)


def first_inner(n_span, part, v, g, jac, codes, src_hbm, pre_hbm, src_in, pre_in, *refs):
    spans = refs[:n_span]
    out, src, pre, ssq_out, sem = refs[n_span:]
    planes = v.shape[1]

    def loads(i):
        return plane_loads(src_hbm, pre_hbm, src, pre, sem, i)

    late = [*range(2, planes - 1), 0, planes - 1]
    for i in late:
        for load in loads(i):
            load.start()

    def put(i, c, sl, a):
        out[(c, i, *sl)] = a

    plane = make_plane(v, g, src, pre, jac, codes, put, spans, spans)

    def inner(i, ssq):
        @pl.when(i > 1)
        def _():
            for load in loads(i):
                load.wait()

        return plane(i, ssq)

    ssq_out[...] = lax.fori_loop(1, part, inner, no_sum())
    for i in late[part - 2 :]:
        for load in loads(i):
            load.wait()


def first_rest(n_span, part, v, g, src, pre, jac, codes, ssq_in, out_in, *refs):
    spans = refs[:n_span]
    out, ssq_out = refs[n_span : n_span + 2]
    span_out = refs[n_span + 2 :]
    planes = v.shape[1]

    def put(i, c, sl, a):
        out[(c, i, *sl)] = a

    plane = make_plane(v, g, src, pre, jac, codes, put, spans, spans)
    ssq_out[...] = lax.fori_loop(part, planes - 1, plane, ssq_in[...])
    for i in range(1, planes - 1):
        for c in range(NV):
            span_rows(out, c, i, span_out, i)


def first_edge(pair, n_span, v, g, src, pre, jac, codes, ssq_in, out_in, halo, *refs):
    spans = refs[:n_span]
    out, ssq_out, face = refs[n_span : n_span + 3]
    span_out = refs[n_span + 3 :]
    planes = v.shape[1]

    def put(i, c, sl, a):
        out[(c, i, *sl)] = a
        face[(c, *sl)] = a

    plane = make_plane(v, g, src, pre, jac, codes, put, spans, spans)
    i, inside, sign = edge_of(pair, planes)
    ssq_out[...] = plane(i, ssq_in[...], inside, halo, halo, sign, partner_at(pair))
    if pair == ORDER[1]:
        for k in range(2):
            at = edge_of(k, planes)[0]
            for c in range(NV):
                span_rows(out, c, at, span_out, k)


def second_inner(n_span, v, g, src, pre, jac, codes, *refs):
    spans, g_spans = refs[:n_span], refs[n_span : 2 * n_span]
    out_hbm, ssq_out, out, sem = refs[2 * n_span :]
    planes = v.shape[1]

    def put(i, c, sl, a):
        out[(c, i, *sl)] = a

    plane = make_plane(v, g, src, pre, jac, codes, put, spans, g_spans)

    def store(i):
        return pltpu.make_async_copy(out.at[:, i], out_hbm.at[:, i], sem.at[i])

    def inner(i, ssq):
        ssq = plane(i, ssq)
        store(i).start()
        return ssq

    ssq_out[...] = lax.fori_loop(1, planes - 1, inner, no_sum())

    def finish(i, carry):
        store(i).wait()
        return carry

    lax.fori_loop(1, planes - 1, finish, 0)


def second_edge(pair, n_span, v, g, src, pre, jac, codes, ssq_in, halo, g_halo, *refs):
    spans, g_spans = refs[:n_span], refs[n_span : 2 * n_span]
    refs = refs[2 * n_span :]
    planes = v.shape[1]
    i, inside, sign = edge_of(pair, planes)
    last = pair == ORDER[1]
    out, ssq_out = refs[-2:]

    def put(i, c, sl, a):
        out[(c, *sl)] = a

    plane = make_plane(v, g, src, pre, jac, codes, put, spans, g_spans, pair)
    ssq = plane(i, ssq_in[...], inside, halo, g_halo, sign, partner_at(pair))
    if not last:
        ssq_out[...] = ssq
        return
    lane = lax.broadcasted_iota(jnp.int32, ssq_out.shape, 1)
    before, now = jnp.sum(refs[0][...]), jnp.sum(ssq)
    ssq_out[...] = jnp.where(lane == 0, before, jnp.where(lane == 1, now, 0.0))


def tail_kernel(cells_all, sums, edge_a, edge_b, result_in, result, rms_hbm, rms, sem):
    ends = face_planes(result.shape[1])
    stores = [
        pltpu.make_async_copy(edge, result.at[:, end], sem.at[k])
        for k, (edge, end) in enumerate(zip((edge_a, edge_b), ends))
    ]
    total = jnp.sum(sums[...], axis=0, keepdims=True)
    for store in stores:
        store.start()
    rms[...] = jnp.sqrt(total / cells_all)[:, : rms.shape[1]]
    stores.append(pltpu.make_async_copy(rms, rms_hbm, sem.at[2]))
    stores[-1].start()
    for store in stores:
        store.wait()


def pairs(count, offset):
    both = []
    for i in range(offset, count - 1, 2):
        both += [(i, i + 1), (i + 1, i)]
    return both


def exchange_pair(face, axis, pair):
    return lax.ppermute(face, axis, pairs(lax.axis_size(axis), pair))


def exchange_stream(face, pair):
    streams, spans = lax.axis_size("stream"), lax.axis_size("span")
    along = dict(pairs(streams, pair))
    across = dict(pairs(spans, 0))
    moves = []
    for i in range(streams):
        for j in range(spans):
            if i in along:
                moves.append((i * spans + j, along[i] * spans + j))
            elif j in across:
                moves.append((i * spans + j, i * spans + across[j]))
    return lax.ppermute(face, ("stream", "span"), moves)


def partner_at(pair):
    at, count = lax.axis_index("stream"), lax.axis_size("stream")
    is_odd = odd("stream")
    other = jnp.where(is_odd, at - 1, at + 1) if pair == 0 else jnp.where(is_odd, at + 1, at - 1)
    return jnp.where((other >= 0) & (other < count), 1.0, 0.0).astype(F32)


def exchange(faces, axis):
    return [exchange_pair(face, axis, pair) for pair, face in enumerate(faces)]


def per_device(adjoint_start, source, flow_state, precond, flux_jac, bc_codes):
    _, planes, rows, lanes = adjoint_start.shape
    n_stream, n_span_all = lax.axis_size("stream"), lax.axis_size("span")
    n_devices = n_stream * n_span_all
    n_span = 1 if n_span_all <= 2 else 2
    cells = planes * rows * lanes
    field = shape(NV, planes, rows, lanes)
    tile = shape(SUB, LANE)
    dma = pltpu.SemaphoreType.DMA
    inner_cost = cost(3000 * cells, 4 * cells, 42 * 4 * cells)
    edge_cost = cost(100 * cells, 0, 42 * cells)

    face = shape(NV + 1, rows, lanes)
    first_face = pl.pallas_call(
        pack_kernel,
        out_shape=face,
        in_specs=[HBM] * 2,
        out_specs=VMEM,
        scratch_shapes=[shape(NV, rows, lanes)] * 2 + [dma((2,))],
        cost_estimate=cost(cells, 0, 8 * cells),
        compiler_params=params(),
        name="pack",
    )(*hold(adjoint_start, flow_state, space=pltpu.HBM))
    streams = [None, None]

    def send(pair, face):
        streams[pair] = exchange_stream(face, pair)

    send(ORDER[0], first_face)
    v = adjoint_start
    load_call = pl.pallas_call(
        functools.partial(load_kernel, n_span),
        out_shape=[
            shape(planes, rows, lanes), field, shape(NV, NV, planes, rows, lanes),
            shape(planes, rows, LANE), shape(3 * NV * NV, SUB, LANE), face,
        ]
        + [shape(NV + 1, planes, 1, lanes)] * n_span,
        in_specs=[VMEM] * 2 + [HBM] * 4,
        out_specs=[VMEM] * (6 + n_span),
        scratch_shapes=[
            shape(NV, 3, NV), pltpu.VMEM((planes, rows), jnp.int32), dma((2,)), dma((2, planes)),
        ],
        cost_estimate=inner_cost,
        compiler_params=params(),
        name="load",
    )
    g, src, pre, codes, jac, second_face, *rows_out = load_call(
        *hold(v, flow_state),
        *hold(source, precond, jnp.transpose(flux_jac, (1, 0, 2)), bc_codes, space=pltpu.HBM),
    )
    send(ORDER[1], second_face)
    spans = exchange(rows_out, "span")

    part = 1 + max((planes - 2) * 5 // 6, 1)
    first_call = pl.pallas_call(
        functools.partial(first_inner, n_span, part),
        out_shape=[field, field, shape(NV, NV, planes, rows, lanes), tile],
        in_specs=[VMEM] * 4 + [HBM] * 2 + [VMEM] * (2 + n_span),
        out_specs=[VMEM] * 4,
        scratch_shapes=[dma((2, planes))],
        input_output_aliases={6: 1, 7: 2},
        cost_estimate=inner_cost,
        compiler_params=params(),
        name="first_inner",
    )
    adjoint, src, pre, ssq = first_call(
        *hold(v, g, jac, codes), *hold(source, precond, space=pltpu.HBM), *hold(src, pre, *spans)
    )

    def first_edge_call(pair, adjoint, ssq):
        n_out = n_span if pair == ORDER[1] else 0
        edge_call = pl.pallas_call(
            functools.partial(first_edge, pair, n_span),
            out_shape=[field, tile, shape(NV, rows, lanes)] + [shape(NV, 2, 1, lanes)] * n_out,
            in_specs=[VMEM] * (9 + n_span),
            out_specs=[VMEM] * (3 + n_out),
            input_output_aliases={7: 0},
            cost_estimate=edge_cost,
            compiler_params=params(),
        )
        adjoint, ssq, face, *rows_out = edge_call(
            *hold(v, g, src, pre, jac, codes, ssq, adjoint, streams[pair], *spans)
        )
        return adjoint, ssq, exchange_stream(face, pair), rows_out

    streams_next = [None, None]
    adjoint, ssq, streams_next[ORDER[0]], _ = first_edge_call(ORDER[0], adjoint, ssq)
    rest_call = pl.pallas_call(
        functools.partial(first_rest, n_span, part),
        out_shape=[field, tile] + [shape(NV, planes, 1, lanes)] * n_span,
        in_specs=[VMEM] * (8 + n_span),
        out_specs=[VMEM] * (2 + n_span),
        input_output_aliases={7: 0},
        cost_estimate=inner_cost,
        compiler_params=params(),
        name="first_rest",
    )
    adjoint, ssq, *rows_out = rest_call(*hold(v, g, src, pre, jac, codes, ssq, adjoint, *spans))
    spans_inner = exchange(rows_out, "span")
    adjoint, ssq, streams_next[ORDER[1]], rows_out = first_edge_call(ORDER[1], adjoint, ssq)
    ssq_first = ssq
    spans_edge = exchange(rows_out, "span")

    second_call = pl.pallas_call(
        functools.partial(second_inner, n_span),
        out_shape=[pltpu.HBM(adjoint_start.shape, F32), tile],
        in_specs=[VMEM] * (6 + 2 * n_span),
        out_specs=[HBM, VMEM],
        scratch_shapes=[field, dma((planes,))],
        cost_estimate=inner_cost,
        compiler_params=params(),
        name="second_inner",
    )
    result, ssq = second_call(*hold(adjoint, g, src, pre, jac, codes, *spans_inner, *spans))

    face = shape(NV, rows, lanes)
    edges = [None, None]
    for pair in ORDER:
        last = pair == ORDER[1]
        edge_call = pl.pallas_call(
            functools.partial(second_edge, pair, n_span),
            out_shape=[face, shape(n_devices, LANE) if last else tile],
            in_specs=[VMEM] * (9 + 2 * n_span + last),
            out_specs=[VMEM] * 2,
            cost_estimate=edge_cost,
            compiler_params=params(),
        )
        edges[pair], ssq = edge_call(
            *hold(adjoint, g, src, pre, jac, codes, ssq, streams_next[pair], streams[pair]),
            *hold(*spans_edge, *spans, *([ssq_first] * last)),
        )
    sums = lax.all_to_all(ssq, ("stream", "span"), 0, 0, tiled=True)
    result, rms = pl.pallas_call(
        functools.partial(tail_kernel, float(NV * cells * n_devices)),
        out_shape=[pltpu.HBM(adjoint_start.shape, F32), pltpu.HBM((1, SWEEPS), F32)],
        in_specs=[VMEM] * 3 + [HBM],
        out_specs=[HBM] * 2,
        scratch_shapes=[shape(1, SWEEPS), dma((3,))],
        input_output_aliases={3: 0},
        compiler_params=params(),
        name="tail",
    )(*hold(sums, *edges), *hold(result, space=pltpu.HBM))
    return (result, rms.reshape(SWEEPS))


def solution(mesh):
    in_specs = (
        P(None, "stream", "span", None),
        P(None, "stream", "span", None),
        P(None, "stream", "span", None),
        P(None, None, "stream", "span", None),
        P(),
        P("stream", "span"),
    )
    out_specs = (P(None, "stream", "span", None), P())

    return jax.shard_map(
        per_device, mesh=mesh, in_specs=in_specs, out_specs=out_specs, check_vma=False
    )
```

```python
import functools

import jax
import jax.numpy as jnp
from jax import lax
from jax.experimental import pallas as pl
from jax.experimental.pallas import tpu as pltpu
from jax.sharding import PartitionSpec as P


NV = 5
SWEEPS = 2
SUB, LANE = 8, 128
F32 = jnp.float32
ORDER = (1, 0)
VMEM = pl.BlockSpec(memory_space=pltpu.VMEM)
HBM = pl.BlockSpec(memory_space=pltpu.HBM)


def shape(*dims):
    return pltpu.VMEM(dims, F32)


def hold(*arrays, space=pltpu.VMEM):
    return [pltpu.with_memory_space_constraint(a, space) for a in arrays]


def params():
    return pltpu.CompilerParams(vmem_limit_bytes=4 << 20)


def cost(flops, transcendentals, bytes_accessed):
    return pl.CostEstimate(
        flops=int(flops), transcendentals=int(transcendentals), bytes_accessed=int(bytes_accessed)
    )


def quarter_speed(rho, m1, m2, m3, p):
    momentum = jnp.sqrt(m1 * m1 + m2 * m2 + m3 * m3)
    return 0.25 * (momentum / rho + jnp.sqrt(1.4 * p / rho))


def odd(axis):
    return lax.rem(lax.axis_index(axis), 2) == 1


def face_planes(planes):
    is_odd = odd("stream")
    return jnp.where(is_odd, 0, planes - 1), jnp.where(is_odd, planes - 1, 0)


def span_rows(field, c, i, out_refs, k):
    is_odd = odd("span")
    last = field.shape[-2] - 1
    at = (i,) if c is None else (c, i)
    to = (k,) if c is None else (c, k)
    head = field[(*at, slice(0, 1))]
    tail = field[(*at, slice(last, last + 1))]
    out_refs[0][to] = jnp.where(is_odd, head, tail)
    if len(out_refs) > 1:
        out_refs[1][to] = jnp.where(is_odd, tail, head)


def fill_face(face, v, flow):
    face[NV] = quarter_speed(*[flow(c) for c in range(NV)])
    for c in range(NV):
        face[c] = v(c)


def pack_kernel(v_hbm, flow_hbm, face, flow_in, v_in, sem):
    end = face_planes(v_hbm.shape[1])[ORDER[0]]
    loads = [
        pltpu.make_async_copy(field.at[:, end], target, sem.at[n])
        for n, (field, target) in enumerate(((flow_hbm, flow_in), (v_hbm, v_in)))
    ]
    for load in loads:
        load.start()
    for load in loads:
        load.wait()
    fill_face(face, lambda c: v_in[c], lambda c: flow_in[c])


def plane_loads(src_hbm, pre_hbm, src, pre, sem, i):
    return (
        pltpu.make_async_copy(src_hbm.at[:, i], src.at[:, i], sem.at[0, i]),
        pltpu.make_async_copy(pre_hbm.at[:, :, i], pre.at[:, :, i], sem.at[1, i]),
    )


def load_kernel(n_span, v, flow, src_hbm, pre_hbm, jac_hbm, bc_hbm, *refs):
    g, src, pre, codes, jac, face = refs[:6]
    spans, (jac_in, bc, small, sem) = refs[6 : 6 + n_span], refs[6 + n_span :]
    planes = v.shape[1]
    tables = [
        pltpu.make_async_copy(jac_hbm, jac_in, small.at[0]),
        pltpu.make_async_copy(bc_hbm, bc, small.at[1]),
    ]
    early = plane_loads(src_hbm, pre_hbm, src, pre, sem, 1)
    for load in [*tables, *early]:
        load.start()
    end = face_planes(planes)[ORDER[1]]
    fill_face(face, lambda c: v[c, end], lambda c: flow[c, end])
    for i in range(planes):
        g[i] = quarter_speed(*[flow[c, i] for c in range(NV)])
        for c in range(NV):
            span_rows(v, c, i, spans, i)
    for i in range(planes):
        span_rows(g, None, i, [span.at[NV] for span in spans], i)
    for load in tables:
        load.wait()
    spread_codes(bc, codes)
    for d in range(3):
        for u in range(NV):
            for c in range(NV):
                jac[(d * NV + u) * NV + c] = jnp.broadcast_to(
                    0.5 * jac_in[u, d : d + 1, c : c + 1], (SUB, LANE)
                )
    for load in early:
        load.wait()


def sweep_plane(i, v, prev, nxt, sign, g, gprev, gnxt, tops, bottoms, src, pre, jac, wall, put, ssq):
    rows_n, lanes_n = v.shape[2] // SUB, v.shape[3] // LANE
    lane = lax.broadcasted_iota(jnp.int32, (SUB, LANE), 1)
    row = lax.broadcasted_iota(jnp.int32, (SUB, LANE), 0)
    first_lane, last_lane = lane == 0, lane == LANE - 1
    first_row, last_row = row == 0, row == SUB - 1
    zero = jnp.zeros((SUB, LANE), F32)

    def at(jb, kb):
        return pl.ds(jb * SUB, SUB), pl.ds(kb * LANE, LANE)

    def shifts(get):
        @functools.cache
        def turned(jb, kb, shift, axis):
            return pltpu.roll(tile(jb, kb), shift % (SUB, LANE)[axis], axis)

        @functools.cache
        def tile(jb, kb):
            return get(*at(jb, kb))

        def shifted(top, bottom, jb, kb):
            before = top(kb) if jb == 0 else turned(jb - 1, kb, 1, 0)
            after = bottom(kb) if jb == rows_n - 1 else turned(jb + 1, kb, -1, 0)
            low = zero if kb == 0 else turned(jb, kb - 1, 1, 1)
            high = zero if kb == lanes_n - 1 else turned(jb, kb + 1, -1, 1)
            return (
                tile(jb, kb),
                jnp.where(first_row, before, turned(jb, kb, 1, 0)),
                jnp.where(last_row, after, turned(jb, kb, -1, 0)),
                jnp.where(first_lane, low, turned(jb, kb, 1, 1)),
                jnp.where(last_lane, high, turned(jb, kb, -1, 1)),
            )

        return shifted

    g_shift = shifts(lambda *sl: g[(i, *sl)])
    v_shift = [shifts(lambda *sl, c=c: v[(c, i, *sl)]) for c in range(NV)]
    total = ssq
    for kb in range(lanes_n):
        for jb in range(rows_n):
            sl = at(jb, kb)
            gs, gu, gd, gl, gr = g_shift(
                functools.partial(tops, NV), functools.partial(bottoms, NV), jb, kb
            )
            coefs = [gs + gprev(*sl), gs if gnxt is None else gs + gnxt(*sl), gs + gu, gs + gd, gs + gl, gs + gr]
            diag = ((coefs[0] + coefs[1]) + (coefs[2] + coefs[3])) + (coefs[4] + coefs[5])
            diffs, owns, res = [], [], []
            for c in range(NV):
                own, up, down, left, right = v_shift[c](
                    functools.partial(tops, c), functools.partial(bottoms, c), jb, kb
                )
                before = prev(c, *sl)
                ends = coefs[0] * before
                across = before
                if nxt is not None:
                    after = nxt(c, *sl)
                    ends = ends + coefs[1] * after
                    across = before - after
                if sign is not None:
                    across = sign * across
                diffs.append((across, up - down, left - right))
                owns.append(own)
                pulls = (
                    ends
                    + (coefs[2] * up + coefs[3] * down)
                ) + (coefs[4] * left + coefs[5] * right)
                res.append(src[(c, i, *sl)] - (diag * own - pulls))
            for c in range(NV):
                r = res[c]
                for d in range(3):
                    for u in range(NV):
                        r = r - jac[(d * NV + u) * NV + c] * diffs[u][d]
                res[c] = r
            if kb == 0:
                code = wall(jb)
                on_wall = first_lane & (code != 1)
                for c in range(NV):
                    t = gs * owns[c]
                    for u in range(NV):
                        t = t + jac[(2 * NV + u) * NV + c] * owns[u]
                    if c == 3:
                        t = jnp.where(code == 0, -t, t)
                    res[c] = res[c] + jnp.where(on_wall, t, zero)
            if nxt is None:
                for c in range(NV):
                    put(c, sl, res[c])
                continue
            for c in range(NV):
                total = total + res[c] * res[c]
            for c in range(NV):
                a = owns[c]
                for u in range(NV):
                    a = a + pre[(u, c, i, *sl)] * res[u]
                put(c, sl, a)
    return total


def finish_plane(i, v, g, pre, jac, partial, halo, g_halo, sign, real, put, ssq):
    for kb in range(v.shape[3] // LANE):
        for jb in range(v.shape[2] // SUB):
            sl = (pl.ds(jb * SUB, SUB), pl.ds(kb * LANE, LANE))
            gh = real * g_halo[(NV, *sl)]
            coef = g[(i, *sl)] + gh
            owns = [v[(c, i, *sl)] for c in range(NV)]
            halos = [real * halo[(c, *sl)] for c in range(NV)]
            turned = [sign * h for h in halos]
            res = []
            for c in range(NV):
                r = partial[(c, *sl)] - (gh * owns[c] - coef * halos[c])
                for u in range(NV):
                    r = r + jac[u * NV + c] * turned[u]
                res.append(r)
                ssq = ssq + r * r
            for c in range(NV):
                a = owns[c]
                for u in range(NV):
                    a = a + pre[(u, c, i, *sl)] * res[u]
                put(c, sl, a)
    return ssq


def spread_codes(bc, codes):
    planes, columns = bc.shape
    eye = lax.broadcasted_iota(jnp.int32, (columns, columns), 0) == lax.broadcasted_iota(
        jnp.int32, (columns, columns), 1
    )
    for i in range(planes):
        own = jnp.broadcast_to(bc[i : i + 1, :].astype(F32), (columns, columns))
        column = jnp.sum(jnp.where(eye, own, 0.0), axis=1, keepdims=True)
        codes[i] = jnp.broadcast_to(column, (columns, LANE))


def pick(is_odd, pair, even_ref, idx):
    if len(pair) == 1:
        keep = is_odd if even_ref == 1 else jnp.logical_not(is_odd)
        return jnp.where(keep, pair[0][idx], 0.0)
    return jnp.where(is_odd, pair[1 - even_ref][idx], pair[even_ref][idx])


def make_plane(v, g, src, pre, jac, codes, put, spans, g_spans, span_at=None):
    span_odd = odd("span")

    def rows_of(even_ref, i):
        def get(c, kb):
            pair = g_spans if c == NV else spans
            k = i if c == NV or span_at is None else span_at
            one = pick(span_odd, pair, even_ref, (c, k, slice(None), pl.ds(kb * LANE, LANE)))
            return jnp.broadcast_to(one, (SUB, LANE))

        return get

    def plane(i, ssq, inside=None, halo=None, g_halo=None, sign=None, real=None):
        if inside is None:
            prev = lambda c, *sl: v[(c, i - 1, *sl)]
            nxt = lambda c, *sl: v[(c, i + 1, *sl)]
            gprev = lambda *sl: g[(i - 1, *sl)]
            gnxt = lambda *sl: g[(i + 1, *sl)]
        else:
            prev = lambda c, *sl: v[(c, inside, *sl)]
            nxt = None if halo is None else lambda c, *sl: real * halo[(c, *sl)]
            gprev = lambda *sl: g[(inside, *sl)]
            gnxt = None if halo is None else lambda *sl: real * g_halo[(NV, *sl)]
        return sweep_plane(
            i, v, prev, nxt, sign, g, gprev, gnxt, rows_of(1, i), rows_of(0, i), src, pre, jac,
            lambda jb: codes[i, pl.ds(jb * SUB, SUB), :],
            functools.partial(put, i),
            ssq,
        )

    return plane


def edge_of(pair, planes):
    low = odd("stream") if pair == 0 else jnp.logical_not(odd("stream"))
    return (
        jnp.where(low, 0, planes - 1),
        jnp.where(low, 1, planes - 2),
        jnp.where(low, -1.0, 1.0).astype(F32),
    )


def no_sum():
    return jnp.zeros((SUB, LANE), F32)


def first_inner(n_span, part, v, g, jac, codes, src_hbm, pre_hbm, src_in, pre_in, *refs):
    spans = refs[:n_span]
    out, src, pre, ssq_out, sem = refs[n_span:]
    planes = v.shape[1]

    def loads(i):
        return plane_loads(src_hbm, pre_hbm, src, pre, sem, i)

    late = [*range(2, planes - 1), 0, planes - 1]
    for i in late:
        for load in loads(i):
            load.start()

    def put(i, c, sl, a):
        out[(c, i, *sl)] = a

    plane = make_plane(v, g, src, pre, jac, codes, put, spans, spans)

    def inner(i, ssq):
        @pl.when(i > 1)
        def _():
            for load in loads(i):
                load.wait()

        return plane(i, ssq)

    ssq_out[...] = lax.fori_loop(1, part, inner, no_sum())
    for i in late[part - 2 :]:
        for load in loads(i):
            load.wait()


def first_rest(n_span, part, v, g, src, pre, jac, codes, ssq_in, out_in, *refs):
    spans = refs[:n_span]
    out, ssq_out, partial = refs[n_span : n_span + 3]
    span_out = refs[n_span + 3 :]
    planes = v.shape[1]

    def put(i, c, sl, a):
        out[(c, i, *sl)] = a

    def put_partial(i, c, sl, a):
        partial[(c, *sl)] = a

    plane = make_plane(v, g, src, pre, jac, codes, put, spans, spans)
    ssq_out[...] = lax.fori_loop(part, planes - 1, plane, ssq_in[...])
    ahead = make_plane(v, g, src, pre, jac, codes, put_partial, spans, spans)
    i, inside, sign = edge_of(ORDER[1], planes)
    ahead(i, no_sum(), inside, sign=sign)
    for i in range(1, planes - 1):
        for c in range(NV):
            span_rows(out, c, i, span_out, i)


def first_edge(pair, n_span, v, g, src, pre, jac, codes, ssq_in, out_in, halo, *refs):
    spans = refs[:n_span]
    out, ssq_out, face = refs[n_span : n_span + 3]
    span_out = refs[n_span + 3 :]
    planes = v.shape[1]

    def put(i, c, sl, a):
        out[(c, i, *sl)] = a
        face[(c, *sl)] = a

    i, inside, sign = edge_of(pair, planes)
    if pair == ORDER[0]:
        plane = make_plane(v, g, src, pre, jac, codes, put, spans, spans)
        ssq_out[...] = plane(i, ssq_in[...], inside, halo, halo, sign, partner_at(pair))
    else:
        ssq_out[...] = finish_plane(
            i, v, g, pre, jac, src, halo, halo, sign, partner_at(pair),
            functools.partial(put, i), ssq_in[...],
        )
        for k in range(2):
            at = edge_of(k, planes)[0]
            for c in range(NV):
                span_rows(out, c, at, span_out, k)


def second_inner(n_span, v, g, src, pre, jac, codes, *refs):
    spans, g_spans = refs[:n_span], refs[n_span : 2 * n_span]
    out_hbm, ssq_out, out, sem = refs[2 * n_span :]
    planes = v.shape[1]

    def put(i, c, sl, a):
        out[(c, i, *sl)] = a

    plane = make_plane(v, g, src, pre, jac, codes, put, spans, g_spans)

    def store(i):
        return pltpu.make_async_copy(out.at[:, i], out_hbm.at[:, i], sem.at[i])

    def inner(i, ssq):
        ssq = plane(i, ssq)
        store(i).start()
        return ssq

    ssq_out[...] = lax.fori_loop(1, planes - 1, inner, no_sum())

    def finish(i, carry):
        store(i).wait()
        return carry

    lax.fori_loop(1, planes - 1, finish, 0)


def second_edge(pair, n_span, v, g, src, pre, jac, codes, ssq_in, halo, g_halo, *refs):
    spans, g_spans = refs[:n_span], refs[n_span : 2 * n_span]
    refs = refs[2 * n_span :]
    planes = v.shape[1]
    i, inside, sign = edge_of(pair, planes)

    if pair == ORDER[0]:
        out, ssq_out, partial = refs

        def put(i, c, sl, a):
            out[(c, *sl)] = a

        def put_partial(i, c, sl, a):
            partial[(c, *sl)] = a

        plane = make_plane(v, g, src, pre, jac, codes, put, spans, g_spans, pair)
        ssq_out[...] = plane(i, ssq_in[...], inside, halo, g_halo, sign, partner_at(pair))
        other = ORDER[1]
        ahead = make_plane(v, g, src, pre, jac, codes, put_partial, spans, g_spans, other)
        i, inside, sign = edge_of(other, planes)
        ahead(i, no_sum(), inside, sign=sign)
        return

    ssq_before, out, ssq_out = refs

    def put_last(c, sl, a):
        out[(c, *sl)] = a

    ssq = finish_plane(
        i, v, g, pre, jac, src, halo, g_halo, sign, partner_at(pair), put_last, ssq_in[...]
    )
    lane = lax.broadcasted_iota(jnp.int32, ssq_out.shape, 1)
    before, now = jnp.sum(ssq_before[...]), jnp.sum(ssq)
    ssq_out[...] = jnp.where(lane == 0, before, jnp.where(lane == 1, now, 0.0))


def tail_kernel(cells_all, sums, edge_a, edge_b, result_in, result, rms_hbm, rms, sem):
    ends = face_planes(result.shape[1])
    stores = [
        pltpu.make_async_copy(edge, result.at[:, end], sem.at[k])
        for k, (edge, end) in enumerate(zip((edge_a, edge_b), ends))
    ]
    total = jnp.sum(sums[...], axis=0, keepdims=True)
    for store in stores:
        store.start()
    rms[...] = jnp.sqrt(total / cells_all)[:, : rms.shape[1]]
    stores.append(pltpu.make_async_copy(rms, rms_hbm, sem.at[2]))
    stores[-1].start()
    for store in stores:
        store.wait()


def pairs(count, offset):
    both = []
    for i in range(offset, count - 1, 2):
        both += [(i, i + 1), (i + 1, i)]
    return both


def exchange_pair(face, axis, pair):
    return lax.ppermute(face, axis, pairs(lax.axis_size(axis), pair))


def exchange_stream(face, pair):
    streams, spans = lax.axis_size("stream"), lax.axis_size("span")
    along = dict(pairs(streams, pair))
    across = dict(pairs(spans, 0))
    moves = []
    for i in range(streams):
        for j in range(spans):
            if i in along:
                moves.append((i * spans + j, along[i] * spans + j))
            elif j in across:
                moves.append((i * spans + j, i * spans + across[j]))
    return lax.ppermute(face, ("stream", "span"), moves)


def partner_at(pair):
    at, count = lax.axis_index("stream"), lax.axis_size("stream")
    is_odd = odd("stream")
    other = jnp.where(is_odd, at - 1, at + 1) if pair == 0 else jnp.where(is_odd, at + 1, at - 1)
    return jnp.where((other >= 0) & (other < count), 1.0, 0.0).astype(F32)


def exchange(faces, axis):
    return [exchange_pair(face, axis, pair) for pair, face in enumerate(faces)]


def per_device(adjoint_start, source, flow_state, precond, flux_jac, bc_codes):
    _, planes, rows, lanes = adjoint_start.shape
    n_stream, n_span_all = lax.axis_size("stream"), lax.axis_size("span")
    n_devices = n_stream * n_span_all
    n_span = 1 if n_span_all <= 2 else 2
    cells = planes * rows * lanes
    field = shape(NV, planes, rows, lanes)
    tile = shape(SUB, LANE)
    dma = pltpu.SemaphoreType.DMA
    inner_cost = cost(3000 * cells, 4 * cells, 42 * 4 * cells)
    edge_cost = cost(100 * cells, 0, 42 * cells)

    face = shape(NV + 1, rows, lanes)
    first_face = pl.pallas_call(
        pack_kernel,
        out_shape=face,
        in_specs=[HBM] * 2,
        out_specs=VMEM,
        scratch_shapes=[shape(NV, rows, lanes)] * 2 + [dma((2,))],
        cost_estimate=cost(cells, 0, 8 * cells),
        compiler_params=params(),
        name="pack",
    )(*hold(adjoint_start, flow_state, space=pltpu.HBM))
    streams = [None, None]

    def send(pair, face):
        streams[pair] = exchange_stream(face, pair)

    send(ORDER[0], first_face)
    v = adjoint_start
    load_call = pl.pallas_call(
        functools.partial(load_kernel, n_span),
        out_shape=[
            shape(planes, rows, lanes), field, shape(NV, NV, planes, rows, lanes),
            shape(planes, rows, LANE), shape(3 * NV * NV, SUB, LANE), face,
        ]
        + [shape(NV + 1, planes, 1, lanes)] * n_span,
        in_specs=[VMEM] * 2 + [HBM] * 4,
        out_specs=[VMEM] * (6 + n_span),
        scratch_shapes=[
            shape(NV, 3, NV), pltpu.VMEM((planes, rows), jnp.int32), dma((2,)), dma((2, planes)),
        ],
        cost_estimate=inner_cost,
        compiler_params=params(),
        name="load",
    )
    g, src, pre, codes, jac, second_face, *rows_out = load_call(
        *hold(v, flow_state),
        *hold(source, precond, jnp.transpose(flux_jac, (1, 0, 2)), bc_codes, space=pltpu.HBM),
    )
    send(ORDER[1], second_face)
    spans = exchange(rows_out, "span")

    part = 1 + max((planes - 2) * 5 // 6, 1)
    first_call = pl.pallas_call(
        functools.partial(first_inner, n_span, part),
        out_shape=[field, field, shape(NV, NV, planes, rows, lanes), tile],
        in_specs=[VMEM] * 4 + [HBM] * 2 + [VMEM] * (2 + n_span),
        out_specs=[VMEM] * 4,
        scratch_shapes=[dma((2, planes))],
        input_output_aliases={6: 1, 7: 2},
        cost_estimate=inner_cost,
        compiler_params=params(),
        name="first_inner",
    )
    adjoint, src, pre, ssq = first_call(
        *hold(v, g, jac, codes), *hold(source, precond, space=pltpu.HBM), *hold(src, pre, *spans)
    )

    def first_edge_call(pair, src, adjoint, ssq):
        n_out = n_span if pair == ORDER[1] else 0
        edge_call = pl.pallas_call(
            functools.partial(first_edge, pair, n_span),
            out_shape=[field, tile, shape(NV, rows, lanes)] + [shape(NV, 2, 1, lanes)] * n_out,
            in_specs=[VMEM] * (9 + n_span),
            out_specs=[VMEM] * (3 + n_out),
            input_output_aliases={7: 0},
            cost_estimate=edge_cost,
            compiler_params=params(),
        )
        adjoint, ssq, face, *rows_out = edge_call(
            *hold(v, g, src, pre, jac, codes, ssq, adjoint, streams[pair], *spans)
        )
        return adjoint, ssq, exchange_stream(face, pair), rows_out

    streams_next = [None, None]
    adjoint, ssq, streams_next[ORDER[0]], _ = first_edge_call(ORDER[0], src, adjoint, ssq)
    rest_call = pl.pallas_call(
        functools.partial(first_rest, n_span, part),
        out_shape=[field, tile, shape(NV, rows, lanes)] + [shape(NV, planes, 1, lanes)] * n_span,
        in_specs=[VMEM] * (8 + n_span),
        out_specs=[VMEM] * (3 + n_span),
        input_output_aliases={7: 0},
        cost_estimate=inner_cost,
        compiler_params=params(),
        name="first_rest",
    )
    adjoint, ssq, partial, *rows_out = rest_call(*hold(v, g, src, pre, jac, codes, ssq, adjoint, *spans))
    spans_inner = exchange(rows_out, "span")
    adjoint, ssq, streams_next[ORDER[1]], rows_out = first_edge_call(
        ORDER[1], partial, adjoint, ssq
    )
    ssq_first = ssq
    spans_edge = exchange(rows_out, "span")

    second_call = pl.pallas_call(
        functools.partial(second_inner, n_span),
        out_shape=[pltpu.HBM(adjoint_start.shape, F32), tile],
        in_specs=[VMEM] * (6 + 2 * n_span),
        out_specs=[HBM, VMEM],
        scratch_shapes=[field, dma((planes,))],
        cost_estimate=inner_cost,
        compiler_params=params(),
        name="second_inner",
    )
    result, ssq = second_call(*hold(adjoint, g, src, pre, jac, codes, *spans_inner, *spans))

    face = shape(NV, rows, lanes)
    edges = [None, None]
    for pair in ORDER:
        last = pair == ORDER[1]
        edge_call = pl.pallas_call(
            functools.partial(second_edge, pair, n_span),
            out_shape=[face, shape(n_devices, LANE)] if last else [face, tile, face],
            in_specs=[VMEM] * (9 + 2 * n_span + last),
            out_specs=[VMEM] * (2 if last else 3),
            cost_estimate=edge_cost,
            compiler_params=params(),
        )
        edges[pair], ssq, *partial = edge_call(
            *hold(adjoint, g, *(partial if last else [src]), pre, jac, codes, ssq),
            *hold(streams_next[pair], streams[pair]),
            *hold(*spans_edge, *spans, *([ssq_first] * last)),
        )
    sums = lax.all_to_all(ssq, ("stream", "span"), 0, 0, tiled=True)
    result, rms = pl.pallas_call(
        functools.partial(tail_kernel, float(NV * cells * n_devices)),
        out_shape=[pltpu.HBM(adjoint_start.shape, F32), pltpu.HBM((1, SWEEPS), F32)],
        in_specs=[VMEM] * 3 + [HBM],
        out_specs=[HBM] * 2,
        scratch_shapes=[shape(1, SWEEPS), dma((3,))],
        input_output_aliases={3: 0},
        compiler_params=params(),
        name="tail",
    )(*hold(sums, *edges), *hold(result, space=pltpu.HBM))
    return (result, rms.reshape(SWEEPS))


def solution(mesh):
    in_specs = (
        P(None, "stream", "span", None),
        P(None, "stream", "span", None),
        P(None, "stream", "span", None),
        P(None, None, "stream", "span", None),
        P(),
        P("stream", "span"),
    )
    out_specs = (P(None, "stream", "span", None), P())

    return jax.shard_map(
        per_device, mesh=mesh, in_specs=in_specs, out_specs=out_specs, check_vma=False
    )
```

```python
import functools

import jax
import jax.numpy as jnp
from jax import lax
from jax.experimental import pallas as pl
from jax.experimental.pallas import tpu as pltpu
from jax.sharding import PartitionSpec as P


NV = 5
SWEEPS = 2
SUB, LANE = 8, 128
F32 = jnp.float32
ORDER = (1, 0)
VMEM = pl.BlockSpec(memory_space=pltpu.VMEM)
HBM = pl.BlockSpec(memory_space=pltpu.HBM)


def shape(*dims):
    return pltpu.VMEM(dims, F32)


def hold(*arrays, space=pltpu.VMEM):
    return [pltpu.with_memory_space_constraint(a, space) for a in arrays]


def params():
    return pltpu.CompilerParams(vmem_limit_bytes=4 << 20)


def cost(flops, transcendentals, bytes_accessed):
    return pl.CostEstimate(
        flops=int(flops), transcendentals=int(transcendentals), bytes_accessed=int(bytes_accessed)
    )


def quarter_speed(rho, m1, m2, m3, p):
    momentum = jnp.sqrt(m1 * m1 + m2 * m2 + m3 * m3)
    return 0.25 * (momentum / rho + jnp.sqrt(1.4 * p / rho))


def odd(axis):
    return lax.rem(lax.axis_index(axis), 2) == 1


def face_planes(planes):
    is_odd = odd("stream")
    return jnp.where(is_odd, 0, planes - 1), jnp.where(is_odd, planes - 1, 0)


def span_rows(field, c, i, out_refs, k):
    is_odd = odd("span")
    last = field.shape[-2] - 1
    at = (i,) if c is None else (c, i)
    to = (k,) if c is None else (c, k)
    head = field[(*at, slice(0, 1))]
    tail = field[(*at, slice(last, last + 1))]
    out_refs[0][to] = jnp.where(is_odd, head, tail)
    if len(out_refs) > 1:
        out_refs[1][to] = jnp.where(is_odd, tail, head)


def fill_face(face, v, flow):
    face[NV] = quarter_speed(*[flow(c) for c in range(NV)])
    for c in range(NV):
        face[c] = v(c)


def pack_kernel(v_hbm, flow_hbm, face, flow_in, v_in, sem):
    end = face_planes(v_hbm.shape[1])[ORDER[0]]
    loads = [
        pltpu.make_async_copy(field.at[:, end], target, sem.at[n])
        for n, (field, target) in enumerate(((flow_hbm, flow_in), (v_hbm, v_in)))
    ]
    for load in loads:
        load.start()
    for load in loads:
        load.wait()
    fill_face(face, lambda c: v_in[c], lambda c: flow_in[c])


def plane_loads(src_hbm, pre_hbm, src, pre, sem, i):
    return (
        pltpu.make_async_copy(src_hbm.at[:, i], src.at[:, i], sem.at[0, i]),
        pltpu.make_async_copy(pre_hbm.at[:, :, i], pre.at[:, :, i], sem.at[1, i]),
    )


def load_kernel(n_span, v, flow, src_hbm, pre_hbm, jac_hbm, bc_hbm, *refs):
    g, src, pre, codes, jac, face = refs[:6]
    spans, (jac_in, bc, small, sem) = refs[6 : 6 + n_span], refs[6 + n_span :]
    planes = v.shape[1]
    tables = [
        pltpu.make_async_copy(jac_hbm, jac_in, small.at[0]),
        pltpu.make_async_copy(bc_hbm, bc, small.at[1]),
    ]
    early = plane_loads(src_hbm, pre_hbm, src, pre, sem, 1)
    for load in [*tables, *early]:
        load.start()
    end = face_planes(planes)[ORDER[1]]
    fill_face(face, lambda c: v[c, end], lambda c: flow[c, end])
    for i in range(planes):
        g[i] = quarter_speed(*[flow[c, i] for c in range(NV)])
        for c in range(NV):
            span_rows(v, c, i, spans, i)
    for i in range(planes):
        span_rows(g, None, i, [span.at[NV] for span in spans], i)
    for load in tables:
        load.wait()
    spread_codes(bc, codes)
    for d in range(3):
        for u in range(NV):
            for c in range(NV):
                jac[(d * NV + u) * NV + c] = jnp.broadcast_to(
                    0.5 * jac_in[u, d : d + 1, c : c + 1], (SUB, LANE)
                )
    for load in early:
        load.wait()


def sweep_plane(i, v, prev, nxt, sign, g, gprev, gnxt, tops, bottoms, src, pre, jac, wall, put, ssq):
    rows_n, lanes_n = v.shape[2] // SUB, v.shape[3] // LANE
    lane = lax.broadcasted_iota(jnp.int32, (SUB, LANE), 1)
    row = lax.broadcasted_iota(jnp.int32, (SUB, LANE), 0)
    first_lane, last_lane = lane == 0, lane == LANE - 1
    first_row, last_row = row == 0, row == SUB - 1
    zero = jnp.zeros((SUB, LANE), F32)

    def at(jb, kb):
        return pl.ds(jb * SUB, SUB), pl.ds(kb * LANE, LANE)

    def shifts(get):
        @functools.cache
        def turned(jb, kb, shift, axis):
            return pltpu.roll(tile(jb, kb), shift % (SUB, LANE)[axis], axis)

        @functools.cache
        def tile(jb, kb):
            return get(*at(jb, kb))

        def shifted(top, bottom, jb, kb):
            before = top(kb) if jb == 0 else turned(jb - 1, kb, 1, 0)
            after = bottom(kb) if jb == rows_n - 1 else turned(jb + 1, kb, -1, 0)
            low = zero if kb == 0 else turned(jb, kb - 1, 1, 1)
            high = zero if kb == lanes_n - 1 else turned(jb, kb + 1, -1, 1)
            return (
                tile(jb, kb),
                jnp.where(first_row, before, turned(jb, kb, 1, 0)),
                jnp.where(last_row, after, turned(jb, kb, -1, 0)),
                jnp.where(first_lane, low, turned(jb, kb, 1, 1)),
                jnp.where(last_lane, high, turned(jb, kb, -1, 1)),
            )

        return shifted

    g_shift = shifts(lambda *sl: g[(i, *sl)])
    v_shift = [shifts(lambda *sl, c=c: v[(c, i, *sl)]) for c in range(NV)]
    total = ssq
    for kb in range(lanes_n):
        for jb in range(rows_n):
            sl = at(jb, kb)
            gs, gu, gd, gl, gr = g_shift(
                functools.partial(tops, NV), functools.partial(bottoms, NV), jb, kb
            )
            coefs = [gs + gprev(*sl), gs if gnxt is None else gs + gnxt(*sl), gs + gu, gs + gd, gs + gl, gs + gr]
            diag = ((coefs[0] + coefs[1]) + (coefs[2] + coefs[3])) + (coefs[4] + coefs[5])
            diffs, owns, res = [], [], []
            for c in range(NV):
                own, up, down, left, right = v_shift[c](
                    functools.partial(tops, c), functools.partial(bottoms, c), jb, kb
                )
                before = prev(c, *sl)
                ends = coefs[0] * before
                across = before
                if nxt is not None:
                    after = nxt(c, *sl)
                    ends = ends + coefs[1] * after
                    across = before - after
                if sign is not None:
                    across = sign * across
                diffs.append((across, up - down, left - right))
                owns.append(own)
                pulls = (
                    ends
                    + (coefs[2] * up + coefs[3] * down)
                ) + (coefs[4] * left + coefs[5] * right)
                res.append(src[(c, i, *sl)] - (diag * own - pulls))
            for c in range(NV):
                r = res[c]
                for d in range(3):
                    for u in range(NV):
                        r = r - jac[(d * NV + u) * NV + c] * diffs[u][d]
                res[c] = r
            if kb == 0:
                code = wall(jb)
                on_wall = first_lane & (code != 1)
                for c in range(NV):
                    t = gs * owns[c]
                    for u in range(NV):
                        t = t + jac[(2 * NV + u) * NV + c] * owns[u]
                    if c == 3:
                        t = jnp.where(code == 0, -t, t)
                    res[c] = res[c] + jnp.where(on_wall, t, zero)
            if nxt is None:
                for c in range(NV):
                    put(c, sl, res[c])
                continue
            for c in range(NV):
                total = total + res[c] * res[c]
            for c in range(NV):
                a = owns[c]
                for u in range(NV):
                    a = a + pre[(u, c, i, *sl)] * res[u]
                put(c, sl, a)
    return total


def finish_plane(i, v, g, pre, jac, partial, halo, g_halo, sign, real, put, ssq):
    for kb in range(v.shape[3] // LANE):
        for jb in range(v.shape[2] // SUB):
            sl = (pl.ds(jb * SUB, SUB), pl.ds(kb * LANE, LANE))
            gh = real * g_halo[(NV, *sl)]
            coef = g[(i, *sl)] + gh
            owns = [v[(c, i, *sl)] for c in range(NV)]
            halos = [real * halo[(c, *sl)] for c in range(NV)]
            turned = [sign * h for h in halos]
            res = []
            for c in range(NV):
                r = partial[(c, *sl)] - (gh * owns[c] - coef * halos[c])
                for u in range(NV):
                    r = r + jac[u * NV + c] * turned[u]
                res.append(r)
                ssq = ssq + r * r
            for c in range(NV):
                a = owns[c]
                for u in range(NV):
                    a = a + pre[(u, c, i, *sl)] * res[u]
                put(c, sl, a)
    return ssq


def spread_codes(bc, codes):
    planes, columns = bc.shape
    eye = lax.broadcasted_iota(jnp.int32, (columns, columns), 0) == lax.broadcasted_iota(
        jnp.int32, (columns, columns), 1
    )
    for i in range(planes):
        own = jnp.broadcast_to(bc[i : i + 1, :].astype(F32), (columns, columns))
        column = jnp.sum(jnp.where(eye, own, 0.0), axis=1, keepdims=True)
        codes[i] = jnp.broadcast_to(column, (columns, LANE))


def pick(is_odd, pair, even_ref, idx):
    if len(pair) == 1:
        keep = is_odd if even_ref == 1 else jnp.logical_not(is_odd)
        return jnp.where(keep, pair[0][idx], 0.0)
    return jnp.where(is_odd, pair[1 - even_ref][idx], pair[even_ref][idx])


def make_plane(v, g, src, pre, jac, codes, put, spans, g_spans, span_at=None):
    span_odd = odd("span")

    def rows_of(even_ref, i):
        def get(c, kb):
            pair = g_spans if c == NV else spans
            k = i if c == NV or span_at is None else span_at
            one = pick(span_odd, pair, even_ref, (c, k, slice(None), pl.ds(kb * LANE, LANE)))
            return jnp.broadcast_to(one, (SUB, LANE))

        return get

    def plane(i, ssq, inside=None, halo=None, g_halo=None, sign=None, real=None):
        if inside is None:
            prev = lambda c, *sl: v[(c, i - 1, *sl)]
            nxt = lambda c, *sl: v[(c, i + 1, *sl)]
            gprev = lambda *sl: g[(i - 1, *sl)]
            gnxt = lambda *sl: g[(i + 1, *sl)]
        else:
            prev = lambda c, *sl: v[(c, inside, *sl)]
            nxt = None if halo is None else lambda c, *sl: real * halo[(c, *sl)]
            gprev = lambda *sl: g[(inside, *sl)]
            gnxt = None if halo is None else lambda *sl: real * g_halo[(NV, *sl)]
        return sweep_plane(
            i, v, prev, nxt, sign, g, gprev, gnxt, rows_of(1, i), rows_of(0, i), src, pre, jac,
            lambda jb: codes[i, pl.ds(jb * SUB, SUB), :],
            functools.partial(put, i),
            ssq,
        )

    return plane


def edge_of(pair, planes):
    low = odd("stream") if pair == 0 else jnp.logical_not(odd("stream"))
    return (
        jnp.where(low, 0, planes - 1),
        jnp.where(low, 1, planes - 2),
        jnp.where(low, -1.0, 1.0).astype(F32),
    )


def ahead_of(pair, v, g, src, pre, jac, codes, partial, spans, g_spans, span_at=None):
    def put(i, c, sl, a):
        partial[(c, *sl)] = a

    plane = make_plane(v, g, src, pre, jac, codes, put, spans, g_spans, span_at)
    i, inside, sign = edge_of(pair, v.shape[1])
    plane(i, no_sum(), inside, sign=sign)


def no_sum():
    return jnp.zeros((SUB, LANE), F32)


def first_inner(n_span, part, v, g, jac, codes, src_hbm, pre_hbm, src_in, pre_in, *refs):
    spans = refs[:n_span]
    out, src, pre, ssq_out, partial, sem = refs[n_span:]
    planes = v.shape[1]

    def loads(i):
        return plane_loads(src_hbm, pre_hbm, src, pre, sem, i)

    late = [*range(2, planes - 1), 0, planes - 1]
    for i in late:
        for load in loads(i):
            load.start()

    def put(i, c, sl, a):
        out[(c, i, *sl)] = a

    plane = make_plane(v, g, src, pre, jac, codes, put, spans, spans)

    def inner(i, ssq):
        @pl.when(i > 1)
        def _():
            for load in loads(i):
                load.wait()

        return plane(i, ssq)

    ssq_out[...] = lax.fori_loop(1, part, inner, no_sum())
    for i in late[part - 2 :]:
        for load in loads(i):
            load.wait()
    ahead_of(ORDER[0], v, g, src, pre, jac, codes, partial, spans, spans)


def first_rest(n_span, part, v, g, src, pre, jac, codes, ssq_in, out_in, *refs):
    spans = refs[:n_span]
    out, ssq_out, partial = refs[n_span : n_span + 3]
    span_out = refs[n_span + 3 :]
    planes = v.shape[1]

    def put(i, c, sl, a):
        out[(c, i, *sl)] = a

    plane = make_plane(v, g, src, pre, jac, codes, put, spans, spans)
    ssq_out[...] = lax.fori_loop(part, planes - 1, plane, ssq_in[...])
    ahead_of(ORDER[1], v, g, src, pre, jac, codes, partial, spans, spans)
    for i in range(1, planes - 1):
        for c in range(NV):
            span_rows(out, c, i, span_out, i)


def first_edge(pair, v, g, partial, pre, jac, ssq_in, out_in, halo, out, ssq_out, face, *span_out):
    planes = v.shape[1]

    def put(i, c, sl, a):
        out[(c, i, *sl)] = a
        face[(c, *sl)] = a

    i, _, sign = edge_of(pair, planes)
    ssq_out[...] = finish_plane(
        i, v, g, pre, jac, partial, halo, halo, sign, partner_at(pair),
        functools.partial(put, i), ssq_in[...],
    )
    if pair == ORDER[1]:
        for k in range(2):
            at = edge_of(k, planes)[0]
            for c in range(NV):
                span_rows(out, c, at, span_out, k)


def second_inner(n_span, v, g, src, pre, jac, codes, *refs):
    spans, g_spans = refs[:n_span], refs[n_span : 2 * n_span]
    out_hbm, ssq_out, out, sem = refs[2 * n_span :]
    planes = v.shape[1]

    def put(i, c, sl, a):
        out[(c, i, *sl)] = a

    plane = make_plane(v, g, src, pre, jac, codes, put, spans, g_spans)

    def store(i):
        return pltpu.make_async_copy(out.at[:, i], out_hbm.at[:, i], sem.at[i])

    def inner(i, ssq):
        ssq = plane(i, ssq)
        store(i).start()
        return ssq

    ssq_out[...] = lax.fori_loop(1, planes - 1, inner, no_sum())

    def finish(i, carry):
        store(i).wait()
        return carry

    lax.fori_loop(1, planes - 1, finish, 0)


def second_edge(pair, n_span, v, g, src, pre, jac, codes, ssq_in, halo, g_halo, *refs):
    spans, g_spans = refs[:n_span], refs[n_span : 2 * n_span]
    refs = refs[2 * n_span :]
    planes = v.shape[1]
    i, inside, sign = edge_of(pair, planes)

    if pair == ORDER[0]:
        out, ssq_out, partial = refs

        def put(i, c, sl, a):
            out[(c, *sl)] = a

        plane = make_plane(v, g, src, pre, jac, codes, put, spans, g_spans, pair)
        ssq_out[...] = plane(i, ssq_in[...], inside, halo, g_halo, sign, partner_at(pair))
        other = ORDER[1]
        ahead_of(other, v, g, src, pre, jac, codes, partial, spans, g_spans, other)
        return

    ssq_before, out, ssq_out = refs

    def put_last(c, sl, a):
        out[(c, *sl)] = a

    ssq = finish_plane(
        i, v, g, pre, jac, src, halo, g_halo, sign, partner_at(pair), put_last, ssq_in[...]
    )
    lane = lax.broadcasted_iota(jnp.int32, ssq_out.shape, 1)
    before, now = jnp.sum(ssq_before[...]), jnp.sum(ssq)
    ssq_out[...] = jnp.where(lane == 0, before, jnp.where(lane == 1, now, 0.0))


def tail_kernel(cells_all, sums, edge_a, edge_b, result_in, result, rms_hbm, rms, sem):
    ends = face_planes(result.shape[1])
    stores = [
        pltpu.make_async_copy(edge, result.at[:, end], sem.at[k])
        for k, (edge, end) in enumerate(zip((edge_a, edge_b), ends))
    ]
    for store in stores:
        store.start()
    total = jnp.sum(sums[...], axis=0, keepdims=True)
    rms[...] = jnp.sqrt(total / cells_all)[:, : rms.shape[1]]
    stores.append(pltpu.make_async_copy(rms, rms_hbm, sem.at[2]))
    stores[-1].start()
    for store in stores:
        store.wait()


def pairs(count, offset):
    both = []
    for i in range(offset, count - 1, 2):
        both += [(i, i + 1), (i + 1, i)]
    return both


def exchange_pair(face, axis, pair):
    return lax.ppermute(face, axis, pairs(lax.axis_size(axis), pair))


def exchange_stream(face, pair):
    streams, spans = lax.axis_size("stream"), lax.axis_size("span")
    along = dict(pairs(streams, pair))
    across = dict(pairs(spans, 0))
    moves = []
    for i in range(streams):
        for j in range(spans):
            if i in along:
                moves.append((i * spans + j, along[i] * spans + j))
            elif j in across:
                moves.append((i * spans + j, i * spans + across[j]))
    return lax.ppermute(face, ("stream", "span"), moves)


def partner_at(pair):
    at, count = lax.axis_index("stream"), lax.axis_size("stream")
    is_odd = odd("stream")
    other = jnp.where(is_odd, at - 1, at + 1) if pair == 0 else jnp.where(is_odd, at + 1, at - 1)
    return jnp.where((other >= 0) & (other < count), 1.0, 0.0).astype(F32)


def exchange(faces, axis):
    return [exchange_pair(face, axis, pair) for pair, face in enumerate(faces)]


def per_device(adjoint_start, source, flow_state, precond, flux_jac, bc_codes):
    _, planes, rows, lanes = adjoint_start.shape
    n_stream, n_span_all = lax.axis_size("stream"), lax.axis_size("span")
    n_devices = n_stream * n_span_all
    n_span = 1 if n_span_all <= 2 else 2
    cells = planes * rows * lanes
    field = shape(NV, planes, rows, lanes)
    tile = shape(SUB, LANE)
    dma = pltpu.SemaphoreType.DMA
    inner_cost = cost(3000 * cells, 4 * cells, 42 * 4 * cells)
    edge_cost = cost(100 * cells, 0, 42 * cells)

    face = shape(NV + 1, rows, lanes)
    first_face = pl.pallas_call(
        pack_kernel,
        out_shape=face,
        in_specs=[HBM] * 2,
        out_specs=VMEM,
        scratch_shapes=[shape(NV, rows, lanes)] * 2 + [dma((2,))],
        cost_estimate=cost(cells, 0, 8 * cells),
        compiler_params=params(),
        name="pack",
    )(*hold(adjoint_start, flow_state, space=pltpu.HBM))
    streams = [None, None]

    def send(pair, face):
        streams[pair] = exchange_stream(face, pair)

    send(ORDER[0], first_face)
    v = adjoint_start
    load_call = pl.pallas_call(
        functools.partial(load_kernel, n_span),
        out_shape=[
            shape(planes, rows, lanes), field, shape(NV, NV, planes, rows, lanes),
            shape(planes, rows, LANE), shape(3 * NV * NV, SUB, LANE), face,
        ]
        + [shape(NV + 1, planes, 1, lanes)] * n_span,
        in_specs=[VMEM] * 2 + [HBM] * 4,
        out_specs=[VMEM] * (6 + n_span),
        scratch_shapes=[
            shape(NV, 3, NV), pltpu.VMEM((planes, rows), jnp.int32), dma((2,)), dma((2, planes)),
        ],
        cost_estimate=inner_cost,
        compiler_params=params(),
        name="load",
    )
    g, src, pre, codes, jac, second_face, *rows_out = load_call(
        *hold(v, flow_state),
        *hold(source, precond, jnp.transpose(flux_jac, (1, 0, 2)), bc_codes, space=pltpu.HBM),
    )
    send(ORDER[1], second_face)
    spans = exchange(rows_out, "span")

    part = 1 + max((planes - 2) // 2, 1)
    first_call = pl.pallas_call(
        functools.partial(first_inner, n_span, part),
        out_shape=[
            field, field, shape(NV, NV, planes, rows, lanes), tile, shape(NV, rows, lanes),
        ],
        in_specs=[VMEM] * 4 + [HBM] * 2 + [VMEM] * (2 + n_span),
        out_specs=[VMEM] * 5,
        scratch_shapes=[dma((2, planes))],
        input_output_aliases={6: 1, 7: 2},
        cost_estimate=inner_cost,
        compiler_params=params(),
        name="first_inner",
    )
    adjoint, src, pre, ssq, partial = first_call(
        *hold(v, g, jac, codes), *hold(source, precond, space=pltpu.HBM), *hold(src, pre, *spans)
    )

    def first_edge_call(pair, partial, adjoint, ssq):
        n_out = n_span if pair == ORDER[1] else 0
        edge_call = pl.pallas_call(
            functools.partial(first_edge, pair),
            out_shape=[field, tile, shape(NV, rows, lanes)] + [shape(NV, 2, 1, lanes)] * n_out,
            in_specs=[VMEM] * 8,
            out_specs=[VMEM] * (3 + n_out),
            input_output_aliases={6: 0},
            cost_estimate=edge_cost,
            compiler_params=params(),
        )
        adjoint, ssq, face, *rows_out = edge_call(
            *hold(v, g, partial, pre, jac, ssq, adjoint, streams[pair])
        )
        return adjoint, ssq, exchange_stream(face, pair), rows_out

    streams_next = [None, None]
    adjoint, ssq, streams_next[ORDER[0]], _ = first_edge_call(
        ORDER[0], partial, adjoint, ssq
    )
    rest_call = pl.pallas_call(
        functools.partial(first_rest, n_span, part),
        out_shape=[field, tile, shape(NV, rows, lanes)] + [shape(NV, planes, 1, lanes)] * n_span,
        in_specs=[VMEM] * (8 + n_span),
        out_specs=[VMEM] * (3 + n_span),
        input_output_aliases={7: 0},
        cost_estimate=inner_cost,
        compiler_params=params(),
        name="first_rest",
    )
    adjoint, ssq, partial, *rows_out = rest_call(*hold(v, g, src, pre, jac, codes, ssq, adjoint, *spans))
    spans_inner = exchange(rows_out, "span")
    adjoint, ssq, streams_next[ORDER[1]], rows_out = first_edge_call(
        ORDER[1], partial, adjoint, ssq
    )
    ssq_first = ssq
    spans_edge = exchange(rows_out, "span")

    second_call = pl.pallas_call(
        functools.partial(second_inner, n_span),
        out_shape=[pltpu.HBM(adjoint_start.shape, F32), tile],
        in_specs=[VMEM] * (6 + 2 * n_span),
        out_specs=[HBM, VMEM],
        scratch_shapes=[field, dma((planes,))],
        cost_estimate=inner_cost,
        compiler_params=params(),
        name="second_inner",
    )
    result, ssq = second_call(*hold(adjoint, g, src, pre, jac, codes, *spans_inner, *spans))

    face = shape(NV, rows, lanes)
    edges = [None, None]
    for pair in ORDER:
        last = pair == ORDER[1]
        edge_call = pl.pallas_call(
            functools.partial(second_edge, pair, n_span),
            out_shape=[face, shape(n_devices, LANE)] if last else [face, tile, face],
            in_specs=[VMEM] * (9 + 2 * n_span + last),
            out_specs=[VMEM] * (2 if last else 3),
            cost_estimate=edge_cost,
            compiler_params=params(),
        )
        edges[pair], ssq, *partial = edge_call(
            *hold(adjoint, g, *(partial if last else [src]), pre, jac, codes, ssq),
            *hold(streams_next[pair], streams[pair]),
            *hold(*spans_edge, *spans, *([ssq_first] * last)),
        )
    sums = lax.all_to_all(ssq, ("stream", "span"), 0, 0, tiled=True)
    result, rms = pl.pallas_call(
        functools.partial(tail_kernel, float(NV * cells * n_devices)),
        out_shape=[pltpu.HBM(adjoint_start.shape, F32), pltpu.HBM((1, SWEEPS), F32)],
        in_specs=[VMEM] * 3 + [HBM],
        out_specs=[HBM] * 2,
        scratch_shapes=[shape(1, SWEEPS), dma((3,))],
        input_output_aliases={3: 0},
        compiler_params=params(),
        name="tail",
    )(*hold(sums, *edges), *hold(result, space=pltpu.HBM))
    return (result, rms.reshape(SWEEPS))


def solution(mesh):
    in_specs = (
        P(None, "stream", "span", None),
        P(None, "stream", "span", None),
        P(None, "stream", "span", None),
        P(None, None, "stream", "span", None),
        P(),
        P("stream", "span"),
    )
    out_specs = (P(None, "stream", "span", None), P())

    return jax.shard_map(
        per_device, mesh=mesh, in_specs=in_specs, out_specs=out_specs, check_vma=False
    )
```
